256 devices in a mesh: slab: 32 (over x, z), grp: 8 (over y, core).
Axes of the slice: x: 4, y: 4, z: 8, core: 2. Of those that a mesh axis runs over, the one named last changes fastest.
Arguments:
- tile_centres: int32 [3, 8192], P(None, ('slab', 'grp')), may hold values from 0 to 511, as said below
- tile_coeffs: float32 [64, 8192], P(None, ('slab', 'grp')), may hold values from -4 to 4
- tile_exponents: float32 [8192], P(('slab', 'grp')), may hold values from 0.02 to 0.3
- tile_live: int32 [8192], P(('slab', 'grp')), may hold values from 0 to 1, as said below
Outputs:
- spectrum: float32 [2, 256, 512, 256], P(None, 'slab', 'grp')
The draws below stay inside these ranges and needn't reach their ends.
Inputs may be any that keep to these rules, and one draw needn't show every extreme that they name: `tile_centres`: row 0 holds a tile's cell along the first dimension (below 512), row 1 along the second (below 512), row 2 along the third; the third coordinate of tile p lies in [(p // 256) * 8, (p // 256 + 1) * 8). `tile_live`: 1 for a slot that holds a tile, 0 for an empty one.
All inputs are finite; a program needn't handle non-finite values.
Results may differ from the reference program's by a relative error of at most 0.0001.
Values sent between devices are 32-bit elements; how exact they have to be, the bound alone decides.
No kernel may reach another device: no remote copies, remote signals or barrier semaphores. Data moves between devices by JAX's collectives and lax.ppermute only.
A program may use at most 128 MiB of HBM per device.

```python
import math
import jax
import jax.numpy as jnp
from jax import lax

NX = 512
NY = 512
CZ = 8
HALF = 8
NPOW = 4
SLAB_TILES = 256
TILES = 8192
NZ = 256


def draw_tile_centres(key, part):
    key_x, key_y, key_z = jax.random.split(key, 3)
    first_cells = jax.random.randint(key_x, (TILES,), 0, NX)
    second_cells = jax.random.randint(key_y, (TILES,), 0, NY)
    owner = jnp.arange(TILES, dtype=jnp.int32) // SLAB_TILES
    third_cells = owner * CZ + jax.random.randint(key_z, (TILES,), 0, CZ)
    return jnp.stack([first_cells, second_cells, third_cells]).astype(jnp.int32)


def draw_tile_live(key, part):
    owner = jnp.arange(TILES, dtype=jnp.int32) // SLAB_TILES
    levels = jax.random.randint(jax.random.fold_in(key, 7), (TILES,), 0, 4)
    return (levels < 1 + owner % 4).astype(jnp.int32)


def shard_levels(key, dims, cuts, low, high):
    loudness = 1.0
    for axis_at, shards_of in cuts:
        heights = jax.random.uniform(jax.random.fold_in(jax.random.fold_in(key, 6), axis_at), (shards_of,), jnp.float32, low / len(cuts), high / len(cuts))
        loudness = loudness * jnp.repeat(jnp.exp(heights), dims[axis_at] // shards_of).reshape((-1,) + (1,) * (len(dims) - 1 - axis_at))
    return loudness


def bell_draw(own_key, shape, deviation, most, cuts=(), kind=jnp.bfloat16):
    result = jax.random.normal(own_key, shape, jnp.float32) * deviation
    if len(cuts) > 0:
        result = shard_levels(own_key, shape, cuts, -0.22, 0.18) * result
    return jnp.clip(result, min=-most, max=most).astype(kind)


def setup_inputs(seed: int = 0) -> dict:
    keys = jax.random.split(jax.random.key(seed), 5)
    return {
        "tile_centres": draw_tile_centres(jax.random.fold_in(keys[4], 71), 0),
        "tile_coeffs": bell_draw(keys[1], (NPOW * NPOW * NPOW, TILES), 0.5, 4.0, ((1, 256),), jnp.float32),
        "tile_exponents": jnp.clip(jnp.exp(math.log(0.3) - 2.7080503 * jax.random.uniform(keys[2], (TILES,), jnp.float32) ** shard_levels(keys[2], (TILES,), ((0, 256),), -0.2, 0.2)), 0.02, 0.3),
        "tile_live": draw_tile_live(jax.random.fold_in(keys[4], 71), 0),
    }


def powers_of(distance, decay_rate):
    envelope = jnp.exp(-decay_rate * distance * distance)
    scaled = distance / HALF
    return jnp.stack([envelope * scaled ** power for power in range(NPOW)], axis=0)

def fold_axis(padded, axis, length):
    middle = lax.slice_in_dim(padded, HALF, HALF + length, axis=axis)
    low_part = lax.slice_in_dim(padded, 0, HALF, axis=axis)
    high_part = lax.slice_in_dim(padded, HALF + length, length + 2 * HALF, axis=axis)
    widths_high = [(0, 0), (0, 0), (0, 0)]
    widths_low = [(0, 0), (0, 0), (0, 0)]
    widths_high[axis] = (0, length - HALF)
    widths_low[axis] = (length - HALF, 0)
    return middle + jnp.pad(high_part, widths_high) + jnp.pad(low_part, widths_low)

def reference(tile_centres, tile_coeffs, tile_exponents, tile_live):
    weights = tile_coeffs * tile_live.astype(jnp.float32)[None, :]
    span_cells = 2 * HALF + 1
    offsets = jnp.arange(-HALF, HALF + 1).astype(jnp.float32)
    start_grid = jnp.zeros((NX + 2 * HALF, NY + 2 * HALF, NZ + 2 * HALF), jnp.float32)

    def add_tile(tile_index, density):
        profile = powers_of(offsets, tile_exponents[tile_index])
        coef_block = weights[:, tile_index].reshape(NPOW, NPOW, NPOW)
        gauss_cube = jnp.einsum('abc,ai,bj,ck->ijk', coef_block, profile, profile, profile, precision=lax.Precision.HIGHEST)
        corner = tile_centres[:, tile_index].astype(jnp.int32)
        current = lax.dynamic_slice(density, (corner[0], corner[1], corner[2]), (span_cells, span_cells, span_cells))
        return lax.dynamic_update_slice(density, current + gauss_cube, (corner[0], corner[1], corner[2]))
    padded = lax.fori_loop(0, TILES, add_tile, start_grid)
    density = fold_axis(padded, 0, NX)
    density = fold_axis(density, 1, NY)
    density = fold_axis(density, 2, NZ)
    along_x = jnp.fft.rfft(density, axis=0)[:NX // 2]
    both = jnp.fft.fft(along_x, axis=2) / jnp.sqrt(jnp.float32(NX * NZ))
    return jnp.stack([jnp.real(both), jnp.imag(both)]).astype(jnp.float32)
```

```python
import functools
import math

import jax
import jax.numpy as jnp
import numpy as np
from jax import lax
from jax.experimental import pallas as pl
from jax.experimental.pallas import tpu as pltpu
from jax.sharding import PartitionSpec as P

NX = 512
NY = 512
CZ = 8
HALF = 8
NPOW = 4
TERMS = NPOW * NPOW * NPOW
LANES = 128
ROWS = 17
FEAT = 72
CHUNKS = 2
NT = (((1,), (1,)), ((), ()))
F32 = jnp.float32
BF16 = jnp.bfloat16


def split(value):
    high = value.astype(BF16)
    return high, (value - high.astype(F32)).astype(BF16)


def pack_kernel(copies, coeffs_ref, centres_ref, exponents_ref, live_ref, out_ref, block):
    half = coeffs_ref.shape[0] // 2
    block[0:half, 0:TERMS] = coeffs_ref[0:half, :]
    block[0:half, TERMS:] = coeffs_ref[half:, :]
    centres = centres_ref[...].astype(F32)
    alive = live_ref[...] > 0
    width = 2 * half
    block[half : half + 1, 0:width] = exponents_ref[...]
    block[half : half + 1, width : 2 * width] = centres[0:1]
    block[half : half + 1, 2 * width : 3 * width] = jnp.where(alive, centres[1:2], -1.0)
    block[half : half + 1, 3 * width : 4 * width] = centres[2:3]
    value = block[...]
    for copy in range(copies):
        out_ref[copy * ROWS : (copy + 1) * ROWS, :] = value


def pack_tiles(copies, tile_centres, tile_coeffs, tile_exponents, tile_live):
    return pl.pallas_call(
        functools.partial(pack_kernel, copies),
        out_shape=jax.ShapeDtypeStruct((copies * ROWS, LANES), F32),
        scratch_shapes=[pltpu.VMEM((ROWS, LANES), F32)],
        name="pack_tiles",
    )(tile_coeffs.T, tile_centres, tile_exponents[None, :], tile_live[None, :])


def route_kernel(sources, groups, tri_ref, round_ref, tiles_ref, out_ref, rows_ref, table, rank_ref):
    per_row = 16
    side = sources * per_row
    total = 2 * side
    for source in range(sources):
        rows_ref[source * per_row : (source + 1) * per_row, :] = tiles_ref[
            source * ROWS : source * ROWS + per_row, :
        ]
    turned = rows_ref[...].T
    table[0:TERMS, 0:side] = turned[0:TERMS]
    table[0:TERMS, side:total] = turned[TERMS:]
    misc = tiles_ref[pl.ds(per_row, sources, stride=ROWS), :]
    sublane = lax.broadcasted_iota(jnp.int32, (8, LANES), 0)
    lane = lax.broadcasted_iota(jnp.int32, (8, LANES), 1)
    own = lane // per_row == sublane
    table[TERMS:, :] = jnp.zeros((table.shape[0] - TERMS, total), F32)
    for part in range(sources // 8):
        piece = misc[part * 8 : (part + 1) * 8]
        fanned = pltpu.roll(piece, 0, 1, stride=per_row, stride_axis=0)
        for kind in range(4):
            for which in range(2):
                start = kind * 2 * per_row + which * per_row
                moved = pltpu.roll(fanned, LANES - start, 1) if start else fanned
                row = jnp.sum(jnp.where(own, moved, 0.0), axis=0, keepdims=True)
                at = which * side + part * LANES
                table[TERMS + kind : TERMS + kind + 1, at : at + LANES] = row
    centre_y = table[TERMS + 2 : TERMS + 3, :].astype(jnp.int32)
    rows_own = NY // groups
    group = lax.broadcasted_iota(jnp.int32, (groups, 1), 0)
    reach = (centre_y - group * rows_own + HALF) & (NY - 1)
    chosen = (reach < rows_own + 2 * HALF) & (centre_y >= 0)
    tri = tri_ref[...]
    step = tri.shape[0]
    count = jnp.zeros((groups, 1), F32)
    for part in range(total // step):
        picked = chosen[:, part * step : (part + 1) * step]
        marks = jnp.where(picked, 1.0, 0.0)
        before = jnp.dot(marks.astype(BF16), tri, preferred_element_type=F32)
        rank_ref[:, part * step : (part + 1) * step] = jnp.where(picked, before + count, -1.0)
        count = count + jnp.sum(marks, axis=1, keepdims=True)
    base = (round_ref[0] * (CHUNKS * LANES)).astype(F32)
    high, low = split(table[...])
    both = jnp.concatenate([high, low], axis=0)
    depth = table.shape[0]
    most = jnp.max(count)
    slot = lax.broadcasted_iota(jnp.int32, (LANES, total), 0).astype(F32)
    for target in range(groups):
        held = jnp.max(count[target : target + 1]) - base
        ranks = rank_ref[target : target + 1, :] - base
        for chunk in range(CHUNKS):
            at = (target * CHUNKS + chunk) * FEAT

            @pl.when(held > chunk * LANES)
            def _():
                pick = jnp.where(slot + float(chunk * LANES) == ranks, 1.0, 0.0).astype(BF16)
                got = lax.dot_general(both, pick, NT, preferred_element_type=F32)
                out_ref[at : at + FEAT, :] = got[0:FEAT] + got[depth : depth + FEAT]

            @pl.when(held <= chunk * LANES)
            def _():
                out_ref[at : at + FEAT, :] = jnp.zeros((FEAT, LANES), F32)

            out_ref[at + TERMS + 4 : at + TERMS + 5, :] = jnp.full((1, LANES), held, F32)
            out_ref[at + TERMS + 5 : at + TERMS + 6, :] = jnp.full((1, LANES), most, F32)


def route_tiles(sources, groups, tri, round_index, tiles):
    return pl.pallas_call(
        functools.partial(route_kernel, sources, groups),
        in_specs=[
            pl.BlockSpec(memory_space=pltpu.VMEM),
            pl.BlockSpec(memory_space=pltpu.SMEM),
            pl.BlockSpec(memory_space=pltpu.VMEM),
        ],
        out_specs=pl.BlockSpec(memory_space=pltpu.VMEM),
        out_shape=jax.ShapeDtypeStruct((groups * CHUNKS * FEAT, LANES), F32),
        scratch_shapes=[
            pltpu.VMEM((sources * 16, LANES), F32),
            pltpu.VMEM((80, sources * 32), F32),
            pltpu.VMEM((groups, sources * 32), F32),
        ],
        name="route_tiles",
    )(tri, round_index, tiles)


def powers_of(distance, width_rate, allowed):
    envelope = jnp.where(allowed, jnp.exp(-width_rate * distance * distance), 0.0)
    scaled = distance * (1.0 / HALF)
    found = [envelope]
    for _ in range(NPOW - 1):
        found.append(found[-1] * scaled)
    return found


def spectrum_kernel(
    groups, kx_own, depth, place_ref, tiles_ref, wave_high_ref, wave_low_ref,
    out_ref, most_ref, total, lhs, rhs, weights_x, turn_ref,
):
    rows_own = NY // groups
    first_kx = place_ref[0] * kx_own
    first_y = place_ref[1] * rows_own
    span = NPOW * LANES
    scale = 1.0 / math.sqrt(NX * depth)
    kx = first_kx + lax.broadcasted_iota(jnp.int32, (kx_own, LANES), 0)
    theta = kx.astype(F32) * (2.0 * math.pi / NX)
    cosine = [None, jnp.cos(theta)]
    sine = [None, jnp.sin(theta)]
    for d in range(2, HALF + 1):
        cosine.append(cosine[-1] * cosine[1] - sine[-1] * sine[1])
        sine.append(sine[d - 1] * cosine[1] + cosine[d - 1] * sine[1])
    for d in range(1, HALF + 1):
        turn_ref[d - 1] = cosine[d]
        turn_ref[HALF + d - 1] = sine[d]
    total[...] = jnp.zeros_like(total)
    most = jnp.max(tiles_ref[0, 0, TERMS + 5 : TERMS + 6, :])
    for source in range(1, groups):
        most = jnp.maximum(most, jnp.max(tiles_ref[source, 0, TERMS + 5 : TERMS + 6, :]))
    most_ref[0] = most.astype(jnp.int32)

    def block_of(index, carry):
        source = index // CHUNKS
        chunk = index % CHUNKS
        block = tiles_ref.at[source, chunk]
        held = jnp.max(block[TERMS + 4 : TERMS + 5, :]) - (chunk * LANES).astype(F32)

        @pl.when(held > 0.0)
        def _():
            rate = block[TERMS : TERMS + 1, :]
            centre_x = block[TERMS + 1 : TERMS + 2, :].astype(jnp.int32)
            centre_y = block[TERMS + 2 : TERMS + 3, :].astype(jnp.int32)
            centre_z = block[TERMS + 3 : TERMS + 4, :].astype(jnp.int32)
            z_cells = lax.broadcasted_iota(jnp.int32, (depth, LANES), 0)
            off_z = ((z_cells - centre_z + depth // 2) & (depth - 1)) - depth // 2
            along_z = powers_of(off_z.astype(F32), rate, jnp.abs(off_z) <= HALF)
            for third in range(NPOW):
                high, low = split(along_z[third])
                at = third * LANES
                rhs[:, at : at + LANES] = high
                rhs[:, span + at : span + at + LANES] = high
                rhs[:, 2 * span + at : 2 * span + at + LANES] = low
            even_0 = jnp.full((kx_own, LANES), 0.5 * scale, F32)
            even_2 = jnp.zeros((kx_own, LANES), F32)
            odd_1 = jnp.zeros((kx_own, LANES), F32)
            odd_3 = jnp.zeros((kx_own, LANES), F32)
            for d in range(1, HALF + 1):
                scaled = d / HALF
                weight = jnp.exp(rate * (-float(d * d))) * scale
                even = weight * turn_ref[d - 1]
                odd = (weight * scaled) * turn_ref[HALF + d - 1]
                even_0 = even_0 + even
                even_2 = even_2 + even * (scaled * scaled)
                odd_1 = odd_1 + odd
                odd_3 = odd_3 + odd * (scaled * scaled)
            phase = ((kx * centre_x) & (NX - 1)).astype(F32) * (2.0 * math.pi / NX)
            cos_c = jnp.cos(phase) * 2.0
            sin_c = jnp.sin(phase) * 2.0
            for second in range(NPOW):
                for third in range(NPOW):
                    term = second * NPOW + third
                    step = NPOW * NPOW
                    even = block[term : term + 1, :] * even_0
                    even = even + block[2 * step + term : 2 * step + term + 1, :] * even_2
                    odd = block[step + term : step + term + 1, :] * odd_1
                    odd = odd + block[3 * step + term : 3 * step + term + 1, :] * odd_3
                    weights_x[term, 0:kx_own, :] = cos_c * even - sin_c * odd
                    weights_x[term, kx_own:, :] = -(sin_c * even + cos_c * odd)
            y_cells = first_y + lax.broadcasted_iota(jnp.int32, (rows_own, LANES), 0)
            off_y = ((y_cells - centre_y + NY // 2) & (NY - 1)) - NY // 2
            along_y = powers_of(off_y.astype(F32), rate, jnp.abs(off_y) <= HALF)
            for third in range(NPOW):
                at = third * LANES
                for row in range(2 * kx_own):
                    value = weights_x[third, row : row + 1, :] * along_y[0]
                    for second in range(1, NPOW):
                        term = second * NPOW + third
                        value = value + weights_x[term, row : row + 1, :] * along_y[second]
                    high, low = split(value)
                    y_rows = pl.ds(row * rows_own, rows_own)
                    lhs[y_rows, at : at + LANES] = high
                    lhs[y_rows, span + at : span + at + LANES] = low
                    lhs[y_rows, 2 * span + at : 2 * span + at + LANES] = high
            total[...] += lax.dot_general(lhs[...], rhs[...], NT, preferred_element_type=F32)

        return carry

    lax.fori_loop(0, groups * CHUNKS, block_of, 0)
    half = kx_own * rows_own
    real_high, real_low = split(total[0:half])
    imag_high, imag_low = split(total[half:])
    high = jnp.concatenate([real_high, imag_high], axis=1)
    low = jnp.concatenate([real_low, imag_low], axis=1)
    wave_high = wave_high_ref[...]
    found = jnp.dot(high, wave_high, preferred_element_type=F32)
    found = found + jnp.dot(low, wave_high, preferred_element_type=F32)
    found = found + jnp.dot(high, wave_low_ref[...], preferred_element_type=F32)
    out_ref[0:half] = found[:, 0:depth]
    out_ref[half:] = found[:, depth:]


def spectrum_of(groups, kx_own, depth, place, tiles, wave_high, wave_low):
    rows = 2 * kx_own * (NY // groups)
    vmem = pl.BlockSpec(memory_space=pltpu.VMEM)
    smem = pl.BlockSpec(memory_space=pltpu.SMEM)
    return pl.pallas_call(
        functools.partial(spectrum_kernel, groups, kx_own, depth),
        in_specs=[smem, vmem, vmem, vmem],
        out_specs=[vmem, smem],
        out_shape=[
            jax.ShapeDtypeStruct((rows, depth), F32),
            jax.ShapeDtypeStruct((1,), jnp.int32),
        ],
        scratch_shapes=[
            pltpu.VMEM((rows, depth), F32),
            pltpu.VMEM((rows, 3 * NPOW * LANES), BF16),
            pltpu.VMEM((depth, 3 * NPOW * LANES), BF16),
            pltpu.VMEM((NPOW * NPOW, 2 * kx_own, LANES), F32),
            pltpu.VMEM((2 * HALF, kx_own, LANES), F32),
        ],
        compiler_params=pltpu.CompilerParams(vmem_limit_bytes=40 * 2**20),
        name="spectrum_of_tiles",
    )(place, tiles, wave_high, wave_low)


def wave_table(depth):
    cells = np.arange(depth)
    angle = 2.0 * np.pi * (cells[:, None] * cells[None, :] % depth) / depth
    cosine, sine = np.cos(angle), np.sin(angle)
    table = np.block([[cosine, -sine], [sine, cosine]]).astype(np.float32)
    high = table.astype(jnp.bfloat16)
    low = (table - high.astype(np.float32)).astype(jnp.bfloat16)
    return high, low


def local(tile_centres, tile_coeffs, tile_exponents, tile_live):
    slab_count = lax.axis_size("slab")
    grp_count = lax.axis_size("grp")
    depth = CZ * slab_count
    kx_own = NX // 2 // slab_count
    rows_own = NY // grp_count
    place = jnp.stack([lax.axis_index("slab"), lax.axis_index("grp")]).astype(jnp.int32)
    wave_high, wave_low = (jnp.asarray(part) for part in wave_table(depth))
    tri = jnp.asarray(np.triu(np.ones((256, 256), np.float32), 1).astype(jnp.bfloat16))
    packed = pack_tiles(slab_count, tile_centres, tile_coeffs, tile_exponents, tile_live)
    spread = lax.all_to_all(
        packed.reshape(slab_count, 1, ROWS * LANES), "slab", split_axis=0, concat_axis=0, tiled=True
    )
    tiles = spread.reshape(slab_count * ROWS, LANES)

    def one_round(index):
        routed = route_tiles(slab_count, grp_count, tri, index.reshape(1), tiles)
        routed = lax.all_to_all(
            routed.reshape(grp_count, CHUNKS * FEAT, LANES), "grp", split_axis=0, concat_axis=0, tiled=True
        )
        return spectrum_of(
            grp_count, kx_own, depth, place,
            routed.reshape(grp_count, CHUNKS, FEAT, LANES), wave_high, wave_low,
        )

    found, most = one_round(jnp.int32(0))

    def more(state):
        return state[0] * (CHUNKS * LANES) < state[1]

    def again(state):
        index, most, found = state
        return index + 1, most, found + one_round(index)[0]

    found = lax.while_loop(more, again, (jnp.int32(1), most[0], found))[2]
    return found.reshape(2, kx_own, rows_own, depth)


def solution(mesh):
    return jax.shard_map(
        local,
        mesh=mesh,
        in_specs=(
            P(None, ("slab", "grp")),
            P(None, ("slab", "grp")),
            P(("slab", "grp")),
            P(("slab", "grp")),
        ),
        out_specs=P(None, "slab", "grp", None),
        check_vma=False,
    )
```

```python
import functools
import math

import jax
import jax.numpy as jnp
import numpy as np
from jax import lax
from jax.experimental import pallas as pl
from jax.experimental.pallas import tpu as pltpu
from jax.sharding import PartitionSpec as P

NX = 512
NY = 512
CZ = 8
HALF = 8
NPOW = 4
TERMS = NPOW * NPOW * NPOW
LANES = 128
ROWS = 17
FEAT = 72
SLOTS = 96
BLOCK = 56
COUNT_X = 4
NT = (((1,), (1,)), ((), ()))
F32 = jnp.float32
BF16 = jnp.bfloat16


def split(value):
    high = value.astype(BF16)
    return high, (value - high.astype(F32)).astype(BF16)


def pack_kernel(copies, coeffs_ref, centres_ref, exponents_ref, live_ref, out_ref, block):
    half = coeffs_ref.shape[0] // 2
    block[0:half, 0:TERMS] = coeffs_ref[0:half, :]
    block[0:half, TERMS:] = coeffs_ref[half:, :]
    centres = centres_ref[...].astype(F32)
    alive = live_ref[...] > 0
    width = 2 * half
    block[half : half + 1, 0:width] = exponents_ref[...]
    block[half : half + 1, width : 2 * width] = centres[0:1]
    block[half : half + 1, 2 * width : 3 * width] = jnp.where(alive, centres[1:2], -1.0)
    block[half : half + 1, 3 * width : 4 * width] = centres[2:3]
    value = block[...]
    for copy in range(copies):
        out_ref[copy * ROWS : (copy + 1) * ROWS, :] = value


def pack_tiles(copies, tile_centres, tile_coeffs, tile_exponents, tile_live):
    return pl.pallas_call(
        functools.partial(pack_kernel, copies),
        out_shape=jax.ShapeDtypeStruct((copies * ROWS, LANES), F32),
        scratch_shapes=[pltpu.VMEM((ROWS, LANES), F32)],
        name="pack_tiles",
    )(tile_coeffs.T, tile_centres, tile_exponents[None, :], tile_live[None, :])


def route_kernel(sources, groups, tri_ref, scalar_ref, tiles_ref, out_ref, rows_ref, table, rank_ref, count_ref):
    per_row = 16
    side = sources * per_row
    total = 2 * side
    for source in range(sources):
        rows_ref[source * per_row : (source + 1) * per_row, :] = tiles_ref[
            source * ROWS : source * ROWS + per_row, :
        ]
    turned = rows_ref[...].T
    table[0:TERMS, 0:side] = turned[0:TERMS]
    table[0:TERMS, side:total] = turned[TERMS:]
    misc = tiles_ref[pl.ds(per_row, sources, stride=ROWS), :]
    sublane = lax.broadcasted_iota(jnp.int32, (8, LANES), 0)
    lane = lax.broadcasted_iota(jnp.int32, (8, LANES), 1)
    own = lane // per_row == sublane
    table[TERMS:, :] = jnp.zeros((table.shape[0] - TERMS, total), F32)
    for part in range(sources // 8):
        piece = misc[part * 8 : (part + 1) * 8]
        fanned = pltpu.roll(piece, 0, 1, stride=per_row, stride_axis=0)
        for kind in range(4):
            for which in range(2):
                start = kind * 2 * per_row + which * per_row
                moved = pltpu.roll(fanned, LANES - start, 1) if start else fanned
                row = jnp.sum(jnp.where(own, moved, 0.0), axis=0, keepdims=True)
                at = which * side + part * LANES
                table[TERMS + kind : TERMS + kind + 1, at : at + LANES] = row
    centre_y = table[TERMS + 2 : TERMS + 3, :].astype(jnp.int32)
    rows_own = NY // groups
    group = lax.broadcasted_iota(jnp.int32, (groups, 1), 0)
    reach = (centre_y - group * rows_own + HALF) & (NY - 1)
    reach = jnp.where(centre_y >= 0, reach, NY)
    edges = (0, rows_own // 2, rows_own // 2 + 2 * HALF, rows_own + 2 * HALF)
    tri = tri_ref[...]
    step = tri.shape[0]
    marks = []
    for kind in range(3):
        inside = jnp.where((reach >= edges[kind]) & (reach < edges[kind + 1]), 1.0, 0.0)
        for part in range(total // step):
            marks.append(inside[:, part * step : (part + 1) * step])
    before = jnp.dot(jnp.concatenate(marks, axis=0).astype(BF16), tri, preferred_element_type=F32)
    rank_ref[...] = jnp.full(rank_ref.shape, -1.0, F32)
    count = jnp.zeros((groups, 1), F32)
    index = 0
    for kind in range(3):
        for part in range(total // step):
            lanes = slice(part * step, (part + 1) * step)
            found = before[index * groups : (index + 1) * groups] + count
            rank_ref[:, lanes] = jnp.where(marks[index] > 0.0, found, rank_ref[:, lanes])
            count = count + jnp.sum(marks[index], axis=1, keepdims=True)
            index += 1
        count_ref[kind] = jnp.broadcast_to(count, (groups, LANES))
    base = (scalar_ref[0] * SLOTS).astype(F32)
    core = scalar_ref[1]
    high, low = split(table[...])
    both = jnp.concatenate([high, low], axis=0)
    depth = table.shape[0]
    most = jnp.max(count)
    slot = lax.broadcasted_iota(jnp.int32, (LANES, total), 0).astype(F32)
    lane = lax.broadcasted_iota(jnp.int32, (32, LANES), 1)
    rows_y = groups // 2
    for target in range(rows_y):
        own_row = pl.ds(2 * target + core, 1)
        ranks = rank_ref[own_row, :] - base
        pick = jnp.where(slot == ranks, 1.0, 0.0).astype(BF16)
        got = lax.dot_general(both, pick, NT, preferred_element_type=F32)
        got = got[0:FEAT] + got[depth : depth + FEAT]
        first = jnp.where(lane < 64, got[0:32], pltpu.roll(got[32:64], 64, 1))
        rest = [got[16 * q : 16 * q + 16] for q in range(4)]
        quarter = lane[0:16] // 32
        extra = pltpu.roll(rest[0], 64, 1)
        extra = jnp.where(quarter == 1, pltpu.roll(rest[1], 96, 1), extra)
        extra = jnp.where(quarter == 2, rest[2], extra)
        extra = jnp.where(quarter == 3, pltpu.roll(rest[3], 32, 1), extra)
        ends = [jnp.clip(count_ref[kind, own_row, :] - base, 0.0, float(SLOTS)) for kind in range(3)]
        numbers = jnp.concatenate(
            [got[TERMS : TERMS + 4], ends[2], ends[1], ends[0], jnp.full((1, LANES), most, F32)], axis=0
        )
        for copy in range(out_ref.shape[0] // (BLOCK * rows_y)):
            at = (copy * rows_y + target) * BLOCK
            out_ref[at : at + 32, :] = first
            out_ref[at + 32 : at + 48, :] = extra
            out_ref[at + 48 : at + 56, :] = numbers


def route_tiles(sources, targets, groups, tri, scalars, tiles):
    return pl.pallas_call(
        functools.partial(route_kernel, sources, groups),
        in_specs=[
            pl.BlockSpec(memory_space=pltpu.VMEM),
            pl.BlockSpec(memory_space=pltpu.SMEM),
            pl.BlockSpec(memory_space=pltpu.VMEM),
        ],
        out_specs=pl.BlockSpec(memory_space=pltpu.VMEM),
        out_shape=jax.ShapeDtypeStruct((targets * BLOCK, LANES), F32),
        scratch_shapes=[
            pltpu.VMEM((sources * 16, LANES), F32),
            pltpu.VMEM((80, sources * 32), F32),
            pltpu.VMEM((groups, sources * 32), F32),
            pltpu.VMEM((3, groups, LANES), F32),
        ],
        name="route_tiles",
    )(tri, scalars, tiles)


def powers_of(distance, rate):
    square = distance * distance
    envelope = jnp.where(square <= float(HALF * HALF), jnp.exp(square * rate), 0.0)
    scaled = distance * (1.0 / HALF)
    found = [envelope]
    for _ in range(NPOW - 1):
        found.append(found[-1] * scaled)
    return found


def merge_sources(sources, tiles_ref, bins):
    lane = lax.broadcasted_iota(jnp.int32, (8, LANES), 1)
    ends = [jnp.int32(0), jnp.int32(0)]
    for source in range(sources):
        block = tiles_ref.at[source]
        held, upto, start = (
            jnp.max(block[52 + k : 53 + k, :]).astype(jnp.int32) for k in range(3)
        )
        pieces = []
        for row in range(0, 32, 8):
            extra = block[32 + row % 16 : 40 + row % 16, :]
            pieces.append(
                jnp.where(lane < 64, block[row : row + 8, :], pltpu.roll(extra, 64 if row < 16 else 32, 1))
            )
        for row in range(0, 32, 8):
            extra = block[32 + row % 16 : 40 + row % 16, :]
            extra = extra if row < 16 else pltpu.roll(extra, 96, 1)
            pieces.append(jnp.where(lane < 64, pltpu.roll(block[row : row + 8, :], 64, 1), extra))
        pieces.append(block[48:56, :])
        for half, (begin, end) in enumerate(((jnp.int32(0), upto), (start, held))):
            valid = (lane >= begin) & (lane < end)
            column = ends[half] // LANES
            offset = ends[half] % LANES
            shift = (offset - begin + LANES) % LANES
            for part, piece in enumerate(pieces):
                moved = pltpu.roll(jnp.where(valid, piece, 0.0), shift, 1)
                rows = slice(8 * part, 8 * part + 8)
                bins[half, column, rows, :] = jnp.where(lane < offset, bins[half, column, rows, :], moved)
                bins[half, column + 1, rows, :] = jnp.where(lane < offset, moved, 0.0)
            ends[half] = ends[half] + (end - begin)
    return ends


def spectrum_kernel(
    sources, groups, kx_own, depth, place_ref, tiles_ref, wave_high_ref, wave_low_ref,
    out_ref, most_ref, bins, total, lhs_0, lhs_1, rhs_0, rhs_1, weights_0, weights_1, turn_ref, stage, sems,
):
    rows_own = NY // groups
    rows_half = rows_own // 2
    first_kx = place_ref[0] * kx_own
    first_y = place_ref[1] * rows_own
    span = NPOW * LANES
    size = 2 * kx_own * rows_half
    scale = 1.0 / math.sqrt(NX * depth)
    kx = first_kx + lax.broadcasted_iota(jnp.int32, (kx_own, LANES), 0)
    theta = kx.astype(F32) * (2.0 * math.pi / NX)
    cosine = [None, jnp.cos(theta)]
    sine = [None, jnp.sin(theta)]
    for d in range(2, HALF + 1):
        cosine.append(cosine[-1] * cosine[1] - sine[-1] * sine[1])
        sine.append(sine[d - 1] * cosine[1] + cosine[d - 1] * sine[1])
    for d in range(1, HALF + 1):
        turn_ref[d - 1] = cosine[d]
        turn_ref[HALF + d - 1] = sine[d]
    total[...] = jnp.zeros_like(total)
    lhs_1[...] = jnp.zeros_like(lhs_1)
    rhs_1[...] = jnp.zeros_like(rhs_1)
    bins[:, 0] = jnp.zeros((2, FEAT, LANES), F32)
    most = tiles_ref[0, 55:56, :]
    for source in range(1, sources):
        most = jnp.maximum(most, tiles_ref[source, 55:56, :])
    most_ref[0] = jnp.max(most).astype(jnp.int32)
    ends = merge_sources(sources, tiles_ref, bins)
    lower = (ends[0] + LANES - 1) // LANES
    upper = jnp.maximum((ends[1] + LANES - 1) // LANES, 1)
    bins[1, upper] = jnp.zeros((FEAT, LANES), F32)

    def build(index, lhs, rhs, weights_x):
        half = (index >= lower).astype(jnp.int32)
        block = bins.at[half, index - half * lower]
        rate = -block[TERMS : TERMS + 1, :]
        centre_x = block[TERMS + 1 : TERMS + 2, :].astype(jnp.int32)
        centre_y = block[TERMS + 2 : TERMS + 3, :].astype(jnp.int32)
        centre_z = block[TERMS + 3 : TERMS + 4, :].astype(jnp.int32)
        even_0 = jnp.full((kx_own, LANES), 0.5 * scale, F32)
        even_2 = jnp.zeros((kx_own, LANES), F32)
        odd_1 = jnp.zeros((kx_own, LANES), F32)
        odd_3 = jnp.zeros((kx_own, LANES), F32)
        for d in range(1, HALF + 1):
            scaled = d / HALF
            weight = jnp.exp(rate * float(d * d)) * scale
            even = weight * turn_ref[d - 1]
            odd = (weight * scaled) * turn_ref[HALF + d - 1]
            even_0 = even_0 + even
            even_2 = even_2 + even * (scaled * scaled)
            odd_1 = odd_1 + odd
            odd_3 = odd_3 + odd * (scaled * scaled)
        phase = ((kx * centre_x) & (NX - 1)).astype(F32) * (2.0 * math.pi / NX)
        cos_c = jnp.cos(phase) * 2.0
        sin_c = jnp.sin(phase) * 2.0
        for second in range(NPOW):
            for third in range(NPOW):
                term = second * NPOW + third
                step = NPOW * NPOW
                even = block[term : term + 1, :] * even_0
                even = even + block[2 * step + term : 2 * step + term + 1, :] * even_2
                odd = block[step + term : step + term + 1, :] * odd_1
                odd = odd + block[3 * step + term : 3 * step + term + 1, :] * odd_3
                weights_x[term, 0:kx_own, :] = cos_c * even - sin_c * odd
                weights_x[term, kx_own:, :] = -(sin_c * even + cos_c * odd)
        shift_y = centre_y - (first_y + half * rows_half + NY // 2)
        y_cells = lax.broadcasted_iota(jnp.int32, (rows_half, LANES), 0)
        off_y = ((y_cells - shift_y) & (NY - 1)).astype(F32) - float(NY // 2)
        along_y = powers_of(off_y, rate)
        for third in range(NPOW):
            at = third * LANES
            for row in range(2 * kx_own):
                value = weights_x[third, row : row + 1, :] * along_y[0]
                for second in range(1, NPOW):
                    term = second * NPOW + third
                    value = value + weights_x[term, row : row + 1, :] * along_y[second]
                high, low = split(value)
                y_rows = slice(row * rows_half, (row + 1) * rows_half)
                lhs[y_rows, at : at + LANES] = high
                lhs[y_rows, span + at : span + at + LANES] = low
                lhs[y_rows, 2 * span + at : 2 * span + at + LANES] = high
        shift_z = centre_z - depth // 2
        z_cells = lax.broadcasted_iota(jnp.int32, (depth, LANES), 0)
        off_z = ((z_cells - shift_z) & (depth - 1)).astype(F32) - float(depth // 2)
        along_z = powers_of(off_z, rate)
        for third in range(NPOW):
            high, low = split(along_z[third])
            at = third * LANES
            rhs[:, at : at + LANES] = high
            rhs[:, span + at : span + at + LANES] = high
            rhs[:, 2 * span + at : 2 * span + at + LANES] = low

    def multiply(index, lhs, rhs):
        half = (index >= lower).astype(jnp.int32)
        total[half] += lax.dot_general(lhs[...], rhs[...], NT, preferred_element_type=F32)

    def two_blocks(pair, carry):
        multiply(2 * pair - 1, lhs_1, rhs_1)
        build(2 * pair, lhs_0, rhs_0, weights_0)
        multiply(2 * pair, lhs_0, rhs_0)
        build(2 * pair + 1, lhs_1, rhs_1, weights_1)
        return carry

    lax.fori_loop(0, (lower + upper + 1) // 2, two_blocks, 0)
    total[1] += lax.dot_general(lhs_1[...], rhs_1[...], NT, preferred_element_type=F32)
    copies = []
    for half in range(2):
        real_high, real_low = split(total[half, 0 : size // 2])
        imag_high, imag_low = split(total[half, size // 2 :])
        high = jnp.concatenate([real_high, imag_high], axis=1)
        low = jnp.concatenate([real_low, imag_low], axis=1)
        for part in range(2):
            columns = slice(part * depth, (part + 1) * depth)
            wave = wave_high_ref[:, columns]
            found = jnp.dot(high, wave, preferred_element_type=F32)
            found = found + jnp.dot(low, wave, preferred_element_type=F32)
            found = found + jnp.dot(high, wave_low_ref[:, columns], preferred_element_type=F32)
            stage[half, part] = found.reshape(kx_own, rows_half, depth)
            copies.append(
                pltpu.make_async_copy(
                    stage.at[half, part],
                    out_ref.at[part, :, half * rows_half : (half + 1) * rows_half, :],
                    sems.at[half, part],
                )
            )
            copies[-1].start()
    for copy in copies:
        copy.wait()


def spectrum_of(sources, groups, kx_own, depth, place, tiles, wave_high, wave_low):
    rows_own = NY // groups
    rows_half = rows_own // 2
    size = 2 * kx_own * rows_half
    span = 3 * NPOW * LANES
    columns = sources * SLOTS // LANES + 2
    vmem = pl.BlockSpec(memory_space=pltpu.VMEM)
    smem = pl.BlockSpec(memory_space=pltpu.SMEM)
    return pl.pallas_call(
        functools.partial(spectrum_kernel, sources, groups, kx_own, depth),
        in_specs=[smem, vmem, vmem, vmem],
        out_specs=[pl.BlockSpec(memory_space=pltpu.HBM), smem],
        out_shape=[
            jax.ShapeDtypeStruct((2, kx_own, rows_own, depth), F32),
            jax.ShapeDtypeStruct((1,), jnp.int32),
        ],
        scratch_shapes=[
            pltpu.VMEM((2, columns, FEAT, LANES), F32),
            pltpu.VMEM((2, size, depth), F32),
            pltpu.VMEM((size, span), BF16),
            pltpu.VMEM((size, span), BF16),
            pltpu.VMEM((depth, span), BF16),
            pltpu.VMEM((depth, span), BF16),
            pltpu.VMEM((NPOW * NPOW, 2 * kx_own, LANES), F32),
            pltpu.VMEM((NPOW * NPOW, 2 * kx_own, LANES), F32),
            pltpu.VMEM((2 * HALF, kx_own, LANES), F32),
            pltpu.VMEM((2, 2, kx_own, rows_half, depth), F32),
            pltpu.SemaphoreType.DMA((2, 2)),
        ],
        compiler_params=pltpu.CompilerParams(vmem_limit_bytes=40 * 2**20),
        name="spectrum_of_tiles",
    )(place, tiles, wave_high, wave_low)


def wave_table(depth):
    cells = np.arange(depth)
    angle = 2.0 * np.pi * (cells[:, None] * cells[None, :] % depth) / depth
    cosine, sine = np.cos(angle), np.sin(angle)
    table = np.block([[cosine, -sine], [sine, cosine]]).astype(np.float32)
    high = table.astype(jnp.bfloat16)
    low = (table - high.astype(np.float32)).astype(jnp.bfloat16)
    return high, low


def exchange(value, groups):
    return lax.all_to_all(
        value, ("slab", "grp"), split_axis=0, concat_axis=0, tiled=True, axis_index_groups=groups
    )


def local(tile_centres, tile_coeffs, tile_exponents, tile_live):
    slab_count = lax.axis_size("slab")
    grp_count = lax.axis_size("grp")
    slab, grp = lax.axis_index("slab"), lax.axis_index("grp")
    depth = CZ * slab_count
    kx_own = NX // 2 // slab_count
    count_z = slab_count // COUNT_X
    count_y = grp_count // 2

    def device(x, z, y, core):
        return (x * count_z + z) * grp_count + y * 2 + core

    xs, zs, ys, cores = range(COUNT_X), range(count_z), range(count_y), range(2)
    share = [[device(x, z, y, c) for z in zs for c in cores] for x in xs for y in ys]
    spread = [[device(x, z, y, c) for x in xs for y in ys] for z in zs for c in cores]
    sharers, chunks = len(share[0]), len(spread[0])
    place = jnp.stack([slab, grp]).astype(jnp.int32)
    wave_high, wave_low = (jnp.asarray(part) for part in wave_table(depth))
    tri = jnp.asarray(np.triu(np.ones((256, 256), np.float32), 1).astype(jnp.bfloat16))
    packed = pack_tiles(sharers, tile_centres, tile_coeffs, tile_exponents, tile_live)
    tiles = exchange(packed.reshape(sharers, 1, ROWS * LANES), share).reshape(sharers * ROWS, LANES)

    def one_round(index):
        scalars = jnp.stack([index, grp % 2]).astype(jnp.int32)
        routed = route_tiles(sharers, chunks, grp_count, tri, scalars, tiles)
        routed = exchange(routed.reshape(chunks, BLOCK, LANES), spread)
        return spectrum_of(chunks, grp_count, kx_own, depth, place, routed, wave_high, wave_low)

    found, most = one_round(jnp.int32(0))

    def more(state):
        return state[0] * SLOTS < state[1]

    def again(state):
        index, most, found = state
        return index + 1, most, found + one_round(index)[0]

    return lax.while_loop(more, again, (jnp.int32(1), most[0], found))[2]


def solution(mesh):
    return jax.shard_map(
        local,
        mesh=mesh,
        in_specs=(
            P(None, ("slab", "grp")),
            P(None, ("slab", "grp")),
            P(("slab", "grp")),
            P(("slab", "grp")),
        ),
        out_specs=P(None, "slab", "grp", None),
        check_vma=False,
    )
```

```python
import functools
import math

import jax
import jax.numpy as jnp
import numpy as np
from jax import lax
from jax.experimental import pallas as pl
from jax.experimental.pallas import tpu as pltpu
from jax.sharding import PartitionSpec as P

NX = 512
NY = 512
CZ = 8
HALF = 8
NPOW = 4
TERMS = NPOW * NPOW * NPOW
LANES = 128
ROWS = 17
FEAT = 72
SLOTS = 96
BLOCK = 56
COUNT_X = 4
NT = (((1,), (1,)), ((), ()))
F32 = jnp.float32
BF16 = jnp.bfloat16


def split(value):
    high = value.astype(BF16)
    return high, (value - high.astype(F32)).astype(BF16)


def pack_kernel(copies, place_ref, coeffs_ref, centres_ref, exponents_ref, live_ref, out_ref, block):
    half = coeffs_ref.shape[0] // 2
    block[0:half, 0:TERMS] = coeffs_ref[0:half, :]
    block[0:half, TERMS:] = coeffs_ref[half:, :]
    centres = centres_ref[...].astype(F32)
    alive = live_ref[...] > 0
    width = 2 * half
    block[half : half + 1, 0:width] = exponents_ref[...]
    block[half : half + 1, width : 2 * width] = centres[0:1]
    block[half : half + 1, 2 * width : 3 * width] = jnp.where(alive, centres[1:2], -1.0)
    block[half : half + 1, 3 * width : 4 * width] = centres[2:3]
    value = block[...]
    for copy in range(copies):
        out_ref[copy * ROWS : (copy + 1) * ROWS, :] = value


def pack_tiles(copies, place, tile_centres, tile_coeffs, tile_exponents, tile_live):
    vmem = pl.BlockSpec(memory_space=pltpu.VMEM)
    return pl.pallas_call(
        functools.partial(pack_kernel, copies),
        in_specs=[pl.BlockSpec(memory_space=pltpu.SMEM), vmem, vmem, vmem, vmem],
        out_specs=vmem,
        out_shape=jax.ShapeDtypeStruct((copies * ROWS, LANES), F32),
        scratch_shapes=[pltpu.VMEM((ROWS, LANES), F32)],
        name="pack_tiles",
    )(place, tile_coeffs.T, tile_centres, tile_exponents[None, :], tile_live[None, :])


def route_kernel(sources, groups, place_ref, round_ref, tiles_ref, out_ref, rows_ref, table, rank_ref, count_ref):
    per_row = 16
    side = sources * per_row
    total = 2 * side
    for source in range(sources):
        rows_ref[source * per_row : (source + 1) * per_row, :] = tiles_ref[
            source * ROWS : source * ROWS + per_row, :
        ]
    turned = rows_ref[...].T
    table[0:TERMS, 0:side] = turned[0:TERMS]
    table[0:TERMS, side:total] = turned[TERMS:]
    misc = tiles_ref[pl.ds(per_row, sources, stride=ROWS), :]
    sublane = lax.broadcasted_iota(jnp.int32, (8, LANES), 0)
    lane = lax.broadcasted_iota(jnp.int32, (8, LANES), 1)
    own = lane // per_row == sublane
    table[TERMS:, :] = jnp.zeros((table.shape[0] - TERMS, total), F32)
    for part in range(sources // 8):
        piece = misc[part * 8 : (part + 1) * 8]
        fanned = pltpu.roll(piece, 0, 1, stride=per_row, stride_axis=0)
        for kind in range(4):
            for which in range(2):
                start = kind * 2 * per_row + which * per_row
                moved = pltpu.roll(fanned, LANES - start, 1) if start else fanned
                row = jnp.sum(jnp.where(own, moved, 0.0), axis=0, keepdims=True)
                at = which * side + part * LANES
                table[TERMS + kind : TERMS + kind + 1, at : at + LANES] = row
    centre_y = table[TERMS + 2 : TERMS + 3, :].astype(jnp.int32)
    rows_own = NY // groups
    group = lax.broadcasted_iota(jnp.int32, (groups, 1), 0)
    reach = (centre_y - group * rows_own + HALF) & (NY - 1)
    reach = jnp.where(centre_y >= 0, reach, NY)
    edges = (0, rows_own // 2, rows_own // 2 + 2 * HALF, rows_own + 2 * HALF)
    step = 256
    earlier = lax.broadcasted_iota(jnp.int32, (step, step), 0) < lax.broadcasted_iota(jnp.int32, (step, step), 1)
    tri = jnp.where(earlier, 1.0, 0.0).astype(BF16)
    marks = []
    for kind in range(3):
        inside = jnp.where((reach >= edges[kind]) & (reach < edges[kind + 1]), 1.0, 0.0)
        for part in range(total // step):
            marks.append(inside[:, part * step : (part + 1) * step])
    before = jnp.dot(jnp.concatenate(marks, axis=0).astype(BF16), tri, preferred_element_type=F32)
    rank_ref[...] = jnp.full(rank_ref.shape, -1.0, F32)
    count = jnp.zeros((groups, 1), F32)
    index = 0
    for kind in range(3):
        for part in range(total // step):
            lanes = slice(part * step, (part + 1) * step)
            found = before[index * groups : (index + 1) * groups] + count
            rank_ref[:, lanes] = jnp.where(marks[index] > 0.0, found, rank_ref[:, lanes])
            count = count + jnp.sum(marks[index], axis=1, keepdims=True)
            index += 1
        count_ref[kind] = jnp.broadcast_to(count, (groups, LANES))
    base = (round_ref[0] * SLOTS).astype(F32)
    core = place_ref[1] % 2
    high, low = split(table[...])
    both = jnp.concatenate([high, low], axis=0)
    depth = table.shape[0]
    most = jnp.max(count)
    slot = lax.broadcasted_iota(jnp.int32, (LANES, total), 0).astype(F32)
    lane = lax.broadcasted_iota(jnp.int32, (32, LANES), 1)
    rows_y = groups // 2
    for target in range(rows_y):
        own_row = pl.ds(2 * target + core, 1)
        ranks = rank_ref[own_row, :] - base
        pick = jnp.where(slot == ranks, 1.0, 0.0).astype(BF16)
        got = lax.dot_general(both, pick, NT, preferred_element_type=F32)
        got = got[0:FEAT] + got[depth : depth + FEAT]
        first = jnp.where(lane < 64, got[0:32], pltpu.roll(got[32:64], 64, 1))
        rest = [got[16 * q : 16 * q + 16] for q in range(4)]
        quarter = lane[0:16] // 32
        extra = pltpu.roll(rest[0], 64, 1)
        extra = jnp.where(quarter == 1, pltpu.roll(rest[1], 96, 1), extra)
        extra = jnp.where(quarter == 2, rest[2], extra)
        extra = jnp.where(quarter == 3, pltpu.roll(rest[3], 32, 1), extra)
        ends = [jnp.clip(count_ref[kind, own_row, :] - base, 0.0, float(SLOTS)) for kind in range(3)]
        numbers = jnp.concatenate(
            [got[TERMS : TERMS + 4], ends[2], ends[1], ends[0], jnp.full((1, LANES), most, F32)], axis=0
        )
        for copy in range(out_ref.shape[0] // (BLOCK * rows_y)):
            at = (copy * rows_y + target) * BLOCK
            out_ref[at : at + 32, :] = first
            out_ref[at + 32 : at + 48, :] = extra
            out_ref[at + 48 : at + 56, :] = numbers


def route_tiles(sources, targets, groups, place, round_index, tiles):
    return pl.pallas_call(
        functools.partial(route_kernel, sources, groups),
        in_specs=[
            pl.BlockSpec(memory_space=pltpu.SMEM),
            pl.BlockSpec(memory_space=pltpu.SMEM),
            pl.BlockSpec(memory_space=pltpu.VMEM),
        ],
        out_specs=pl.BlockSpec(memory_space=pltpu.VMEM),
        out_shape=jax.ShapeDtypeStruct((targets * BLOCK, LANES), F32),
        scratch_shapes=[
            pltpu.VMEM((sources * 16, LANES), F32),
            pltpu.VMEM((80, sources * 32), F32),
            pltpu.VMEM((groups, sources * 32), F32),
            pltpu.VMEM((3, groups, LANES), F32),
        ],
        name="route_tiles",
    )(place, round_index, tiles)


def powers_of(distance, rate):
    square = distance * distance
    envelope = jnp.where(square <= float(HALF * HALF), jnp.exp(square * rate), 0.0)
    scaled = distance * (1.0 / HALF)
    found = [envelope]
    for _ in range(NPOW - 1):
        found.append(found[-1] * scaled)
    return found


def merge_sources(sources, tiles_ref, bins):
    lane = lax.broadcasted_iota(jnp.int32, (8, LANES), 1)
    first = LANES // 2
    counts = [tiles_ref[pl.ds(52 + k, sources, stride=BLOCK), :] for k in range(3)]
    ends = [jnp.int32(0), jnp.int32(0)]
    open_column = [[jnp.zeros((8, LANES), F32)] * (FEAT // 8) for _ in range(2)]
    for source in range(sources):
        held, upto, start = (
            jnp.max(count[source : source + 1, :]).astype(jnp.int32) for count in counts
        )
        at = source * BLOCK
        pieces = [tiles_ref[at + row : at + row + 8, :] for row in range(0, 32, 8)]
        numbers = tiles_ref[at + 48 : at + 56, :]
        for half, (begin, end) in enumerate(((jnp.int32(0), upto), (start, held))):
            begin, end = jnp.minimum(begin, first), jnp.minimum(end, first)
            column = ends[half] // LANES
            offset = ends[half] % LANES
            shift = (offset - begin + LANES) % LANES
            after = ends[half] + (end - begin)
            kept = lane < offset
            stays = after // LANES == column
            lower = (lane >= begin) & (lane < end)
            upper = (lane >= begin + first) & (lane < end + first)
            other = (shift + first) % LANES
            moved = [pltpu.roll(jnp.where(lower, piece, 0.0), shift, 1) for piece in pieces]
            moved += [pltpu.roll(jnp.where(upper, piece, 0.0), other, 1) for piece in pieces]
            moved.append(pltpu.roll(jnp.where(lower, numbers, 0.0), shift, 1))
            for part, piece in enumerate(moved):
                full = jnp.where(kept, open_column[half][part], piece)
                bins[half, column, 8 * part : 8 * part + 8, :] = full
                wrapped = jnp.where(kept, piece, 0.0)
                open_column[half][part] = jnp.where(stays, full, wrapped)
            ends[half] = after
    for half in range(2):
        for part in range(FEAT // 8):
            bins[half, ends[half] // LANES, 8 * part : 8 * part + 8, :] = open_column[half][part]

    def rest(source, ends):
        at = pl.multiple_of(source * BLOCK, 8)
        numbers = tiles_ref[pl.ds(at + 48, 8), :]
        held, upto, start = (jnp.max(numbers[4 + k : 5 + k]).astype(jnp.int32) for k in range(3))

        def append(ends):
            lines = [tiles_ref[pl.ds(at + 32 + row, 8), :] for row in (0, 8)]
            result = []
            for half, (begin, end) in enumerate(((jnp.int32(0), upto), (start, held))):
                begin, end = jnp.maximum(begin, first) - first, jnp.maximum(end, first) - first
                column = ends[half] // LANES
                offset = ends[half] % LANES
                kept = lane < offset
                moved = []
                for quarter in range(4):
                    valid = (lane >= begin + 32 * quarter) & (lane < end + 32 * quarter)
                    shift = (offset - begin - 32 * quarter + 2 * LANES) % LANES
                    moved += [pltpu.roll(jnp.where(valid, line, 0.0), shift, 1) for line in lines]
                valid = (lane >= begin + first) & (lane < end + first)
                shift = (offset - begin - first + 2 * LANES) % LANES
                moved.append(pltpu.roll(jnp.where(valid, numbers, 0.0), shift, 1))
                for part, piece in enumerate(moved):
                    rows = slice(8 * part, 8 * part + 8)
                    bins[half, column, rows, :] = jnp.where(kept, bins[half, column, rows, :], piece)
                    bins[half, column + 1, rows, :] = jnp.where(kept, piece, 0.0)
                result.append(ends[half] + end - begin)
            return tuple(result)

        return lax.cond(held > first, append, lambda ends: ends, ends)

    return lax.fori_loop(0, sources, rest, tuple(ends))


def spectrum_kernel(
    sources, groups, kx_own, depth, later, place_ref, tiles_ref, wave, *refs
):
    if later:
        before_ref, *refs = refs
    out_ref, most_ref, bins, total, *refs = refs
    lhs_0, lhs_1, rhs_0, rhs_1, weights_0, weights_1, turn_ref, stage, sems = refs
    rows_own = NY // groups
    rows_half = rows_own // 2
    first_kx = place_ref[0] * kx_own
    first_y = place_ref[1] * rows_own
    size = 2 * kx_own * rows_half
    scale = 1.0 / math.sqrt(NX * depth)
    kx = first_kx + lax.broadcasted_iota(jnp.int32, (kx_own, LANES), 0)
    theta = kx.astype(F32) * (2.0 * math.pi / NX)
    cosine = [None, jnp.cos(theta)]
    sine = [None, jnp.sin(theta)]
    for d in range(2, HALF + 1):
        cosine.append(cosine[-1] * cosine[1] - sine[-1] * sine[1])
        sine.append(sine[d - 1] * cosine[1] + cosine[d - 1] * sine[1])
    for d in range(1, HALF + 1):
        turn_ref[d - 1] = cosine[d]
        turn_ref[HALF + d - 1] = sine[d]
    total[...] = jnp.zeros_like(total)
    lhs_1[...] = jnp.zeros_like(lhs_1)
    rhs_1[...] = jnp.zeros_like(rhs_1)
    most_ref[0] = jnp.max(tiles_ref[pl.ds(55, sources, stride=BLOCK), :]).astype(jnp.int32)
    most_ref[1] = jnp.int32(1)
    ends = merge_sources(sources, tiles_ref, bins)
    lower = (ends[0] + LANES - 1) // LANES
    upper = jnp.maximum((ends[1] + LANES - 1) // LANES, 1)

    def build(index, lhs, rhs, weights_x):
        half = (index >= lower).astype(jnp.int32)
        block = bins.at[half, index - half * lower]
        rate = -block[TERMS : TERMS + 1, :]
        centre_x = block[TERMS + 1 : TERMS + 2, :].astype(jnp.int32)
        centre_y = block[TERMS + 2 : TERMS + 3, :].astype(jnp.int32)
        centre_z = block[TERMS + 3 : TERMS + 4, :].astype(jnp.int32)
        even_0 = jnp.full((kx_own, LANES), 0.5 * scale, F32)
        even_2 = jnp.zeros((kx_own, LANES), F32)
        odd_1 = jnp.zeros((kx_own, LANES), F32)
        odd_3 = jnp.zeros((kx_own, LANES), F32)
        for d in range(1, HALF + 1):
            scaled = d / HALF
            weight = jnp.exp(rate * float(d * d)) * scale
            even = weight * turn_ref[d - 1]
            odd = (weight * scaled) * turn_ref[HALF + d - 1]
            even_0 = even_0 + even
            even_2 = even_2 + even * (scaled * scaled)
            odd_1 = odd_1 + odd
            odd_3 = odd_3 + odd * (scaled * scaled)
        phase = ((kx * centre_x) & (NX - 1)).astype(F32) * (2.0 * math.pi / NX)
        cos_c = jnp.cos(phase) * 2.0
        sin_c = jnp.sin(phase) * 2.0
        for second in range(NPOW):
            for third in range(NPOW):
                term = second * NPOW + third
                step = NPOW * NPOW
                even = block[term : term + 1, :] * even_0
                even = even + block[2 * step + term : 2 * step + term + 1, :] * even_2
                odd = block[step + term : step + term + 1, :] * odd_1
                odd = odd + block[3 * step + term : 3 * step + term + 1, :] * odd_3
                weights_x[term, 0:kx_own, :] = cos_c * even - sin_c * odd
                weights_x[term, kx_own:, :] = -(sin_c * even + cos_c * odd)
        shift_y = centre_y - (first_y + half * rows_half + NY // 2)
        y_cells = lax.broadcasted_iota(jnp.int32, (rows_half, LANES), 0)
        off_y = ((y_cells - shift_y) & (NY - 1)).astype(F32) - float(NY // 2)
        along_y = powers_of(off_y, rate)
        for third in range(NPOW):
            for row in range(2 * kx_own):
                value = weights_x[third, row : row + 1, :] * along_y[0]
                for second in range(1, NPOW):
                    term = second * NPOW + third
                    value = value + weights_x[term, row : row + 1, :] * along_y[second]
                high, low = split(value)
                y_rows = slice(row * rows_half, (row + 1) * rows_half)
                lhs[third, y_rows, :] = high
                lhs[NPOW + third, y_rows, :] = low
        shift_z = centre_z - depth // 2
        z_cells = lax.broadcasted_iota(jnp.int32, (depth, LANES), 0)
        off_z = ((z_cells - shift_z) & (depth - 1)).astype(F32) - float(depth // 2)
        along_z = powers_of(off_z, rate)
        for third in range(NPOW):
            high, low = split(along_z[third])
            rhs[third] = high
            rhs[NPOW + third] = low

    def product(lhs, rhs):
        highs, lows = range(NPOW), range(NPOW, 2 * NPOW)
        left = jnp.concatenate([lhs[k] for k in (*highs, *lows, *highs)], axis=1)
        right = jnp.concatenate([rhs[k] for k in (*highs, *highs, *lows)], axis=1)
        return lax.dot_general(left, right, NT, preferred_element_type=F32)

    def multiply(index, lhs, rhs):
        half = (index >= lower).astype(jnp.int32)
        total[half] += product(lhs, rhs)

    def two_blocks(pair, carry):
        multiply(2 * pair - 1, lhs_1, rhs_1)
        build(2 * pair, lhs_0, rhs_0, weights_0)
        multiply(2 * pair, lhs_0, rhs_0)
        build(2 * pair + 1, lhs_1, rhs_1, weights_1)
        return carry

    blocks = lower + upper
    lax.fori_loop(0, blocks // 2, two_blocks, 0)
    @pl.when(blocks % 2 == 0)
    def _():
        total[1] += product(lhs_1, rhs_1)

    @pl.when(blocks % 2 == 1)
    def _():
        multiply(blocks - 2, lhs_1, rhs_1)
        build(blocks - 1, lhs_0, rhs_0, weights_0)
        total[1] += product(lhs_0, rhs_0)

    parts = []
    for half in range(2):
        real_high, real_low = split(total[half, 0 : size // 2])
        imag_high, imag_low = split(total[half, size // 2 :])
        high = jnp.concatenate([real_high, imag_high], axis=1)
        low = jnp.concatenate([real_low, imag_low], axis=1)
        parts.append((high, low))
    for part in range(2):
        if later:
            pltpu.sync_copy(before_ref.at[part], stage.at[part])
        columns = slice(part * depth, (part + 1) * depth)
        for half, (high, low) in enumerate(parts):
            found = jnp.dot(high, wave[0, :, columns], preferred_element_type=F32)
            found = found + jnp.dot(low, wave[0, :, columns], preferred_element_type=F32)
            found = found + jnp.dot(high, wave[1, :, columns], preferred_element_type=F32)
            found = found.reshape(kx_own, rows_half, depth)
            rows = slice(half * rows_half, (half + 1) * rows_half)
            if later:
                found = found + stage[part, :, rows, :]
            stage[part, :, rows, :] = found
        pltpu.make_async_copy(stage.at[part], out_ref.at[part], sems.at[part]).start()
    for part in range(2):
        pltpu.make_async_copy(stage.at[part], out_ref.at[part], sems.at[part]).wait()


def spectrum_of(sources, groups, kx_own, depth, place, tiles, wave, before=None):
    rows_own = NY // groups
    size = kx_own * rows_own
    columns = sources * SLOTS // LANES + 2
    vmem = pl.BlockSpec(memory_space=pltpu.VMEM)
    smem = pl.BlockSpec(memory_space=pltpu.SMEM)
    hbm = pl.BlockSpec(memory_space=pltpu.HBM)
    later = before is not None
    return pl.pallas_call(
        functools.partial(spectrum_kernel, sources, groups, kx_own, depth, later),
        in_specs=[smem, vmem, vmem] + [hbm] * later,
        out_specs=[hbm, smem],
        out_shape=[
            jax.ShapeDtypeStruct((2, kx_own, rows_own, depth), F32),
            jax.ShapeDtypeStruct((2,), jnp.int32),
        ],
        input_output_aliases={3: 0} if later else {},
        scratch_shapes=[
            pltpu.VMEM((2, columns, FEAT, LANES), F32),
            pltpu.VMEM((2, size, depth), F32),
            pltpu.VMEM((2 * NPOW, size, LANES), BF16),
            pltpu.VMEM((2 * NPOW, size, LANES), BF16),
            pltpu.VMEM((2 * NPOW, depth, LANES), BF16),
            pltpu.VMEM((2 * NPOW, depth, LANES), BF16),
            pltpu.VMEM((NPOW * NPOW, 2 * kx_own, LANES), F32),
            pltpu.VMEM((NPOW * NPOW, 2 * kx_own, LANES), F32),
            pltpu.VMEM((2 * HALF, kx_own, LANES), F32),
            pltpu.VMEM((2, kx_own, rows_own, depth), F32),
            pltpu.SemaphoreType.DMA((2,)),
        ],
        compiler_params=pltpu.CompilerParams(vmem_limit_bytes=40 * 2**20),
        name="spectrum_of_tiles",
    )(place, tiles, wave, *([before] if later else []))


def wave_table(depth):
    cells = np.arange(depth)
    angle = 2.0 * np.pi * (cells[:, None] * cells[None, :] % depth) / depth
    cosine, sine = np.cos(angle), np.sin(angle)
    table = np.block([[cosine, -sine], [sine, cosine]]).astype(np.float32)
    high = table.astype(jnp.bfloat16)
    low = (table - high.astype(np.float32)).astype(jnp.bfloat16)
    return np.stack([high, low])


def exchange(value, groups):
    return lax.all_to_all(
        value, ("slab", "grp"), split_axis=0, concat_axis=0, tiled=True, axis_index_groups=groups
    )


def local(tile_centres, tile_coeffs, tile_exponents, tile_live):
    slab_count = lax.axis_size("slab")
    grp_count = lax.axis_size("grp")
    slab, grp = lax.axis_index("slab"), lax.axis_index("grp")
    depth = CZ * slab_count
    kx_own = NX // 2 // slab_count
    count_z = slab_count // COUNT_X
    count_y = grp_count // 2

    def device(x, z, y, core):
        return (x * count_z + z) * grp_count + y * 2 + core

    xs, zs, ys, cores = range(COUNT_X), range(count_z), range(count_y), range(2)
    share = [[device(x, z, y, c) for z in zs for c in cores] for x in xs for y in ys]
    spread = [[device(x, z, y, c) for x in xs for y in ys] for z in zs for c in cores]
    sharers, chunks = len(share[0]), len(spread[0])
    place = jnp.stack([slab, grp]).astype(jnp.int32)
    wave = jnp.asarray(wave_table(depth))
    packed = pack_tiles(sharers, place, tile_centres, tile_coeffs, tile_exponents, tile_live)
    tiles = exchange(packed.reshape(sharers, 1, ROWS * LANES), share).reshape(sharers * ROWS, LANES)

    def one_round(index, before=None):
        routed = route_tiles(sharers, chunks, grp_count, place, index.reshape(1), tiles)
        routed = exchange(routed.reshape(chunks, BLOCK, LANES), spread).reshape(chunks * BLOCK, LANES)
        return spectrum_of(chunks, grp_count, kx_own, depth, place, routed, wave, before)

    found, most = one_round(jnp.int32(0))

    def more(state):
        return state[0] * SLOTS < state[1]

    def again(state):
        index, most, found = state
        return index + 1, most, one_round(index, found)[0]

    return lax.while_loop(more, again, (most[1], most[0], found))[2]


def solution(mesh):
    return jax.shard_map(
        local,
        mesh=mesh,
        in_specs=(
            P(None, ("slab", "grp")),
            P(None, ("slab", "grp")),
            P(("slab", "grp")),
            P(("slab", "grp")),
        ),
        out_specs=P(None, "slab", "grp", None),
        check_vma=False,
    )
```

```python
import functools
import math

import jax
import jax.numpy as jnp
import numpy as np
from jax import lax
from jax.experimental import pallas as pl
from jax.experimental.pallas import tpu as pltpu
from jax.sharding import PartitionSpec as P

NX = 512
NY = 512
CZ = 8
HALF = 8
NPOW = 4
TERMS = NPOW * NPOW * NPOW
LANES = 128
ROWS = 17
FEAT = 72
SLOTS = 96
BLOCK = 56
COUNT_X = 4
NT = (((1,), (1,)), ((), ()))
F32 = jnp.float32
BF16 = jnp.bfloat16


def split(value):
    high = value.astype(BF16)
    return high, (value - high.astype(F32)).astype(BF16)


def pack_kernel(copies, coeffs_ref, centres_ref, exponents_ref, live_ref, out_ref, block):
    half = coeffs_ref.shape[0] // 2
    block[0:half, 0:TERMS] = coeffs_ref[0:half, :]
    block[0:half, TERMS:] = coeffs_ref[half:, :]
    centres = centres_ref[...].astype(F32)
    alive = live_ref[...] > 0
    width = 2 * half
    block[half : half + 1, 0:width] = exponents_ref[...]
    block[half : half + 1, width : 2 * width] = centres[0:1]
    block[half : half + 1, 2 * width : 3 * width] = jnp.where(alive, centres[1:2], -1.0)
    block[half : half + 1, 3 * width : 4 * width] = centres[2:3]
    value = block[...]
    for copy in range(copies):
        out_ref[copy * ROWS : (copy + 1) * ROWS, :] = value


def pack_tiles(copies, tile_centres, tile_coeffs, tile_exponents, tile_live):
    return pl.pallas_call(
        functools.partial(pack_kernel, copies),
        out_shape=jax.ShapeDtypeStruct((copies * ROWS, LANES), F32),
        scratch_shapes=[pltpu.VMEM((ROWS, LANES), F32)],
        name="pack_tiles",
    )(tile_coeffs.T, tile_centres, tile_exponents[None, :], tile_live[None, :])


def route_kernel(sources, groups, place_ref, round_ref, tiles_ref, out_ref, rows_ref, table, rank_ref, count_ref):
    per_row = 16
    side = sources * per_row
    total = 2 * side
    for source in range(sources):
        rows_ref[source * per_row : (source + 1) * per_row, :] = tiles_ref[
            source * ROWS : source * ROWS + per_row, :
        ]
    turned = rows_ref[...].T
    table[0:TERMS, 0:side] = turned[0:TERMS]
    table[0:TERMS, side:total] = turned[TERMS:]
    misc = tiles_ref[pl.ds(per_row, sources, stride=ROWS), :]
    sublane = lax.broadcasted_iota(jnp.int32, (8, LANES), 0)
    lane = lax.broadcasted_iota(jnp.int32, (8, LANES), 1)
    own = lane // per_row == sublane
    table[TERMS:, :] = jnp.zeros((table.shape[0] - TERMS, total), F32)
    for part in range(sources // 8):
        piece = misc[part * 8 : (part + 1) * 8]
        fanned = pltpu.roll(piece, 0, 1, stride=per_row, stride_axis=0)
        for kind in range(4):
            for which in range(2):
                start = kind * 2 * per_row + which * per_row
                moved = pltpu.roll(fanned, LANES - start, 1) if start else fanned
                row = jnp.sum(jnp.where(own, moved, 0.0), axis=0, keepdims=True)
                at = which * side + part * LANES
                table[TERMS + kind : TERMS + kind + 1, at : at + LANES] = row
    centre_y = table[TERMS + 2 : TERMS + 3, :].astype(jnp.int32)
    rows_own = NY // groups
    group = lax.broadcasted_iota(jnp.int32, (groups, 1), 0)
    reach = (centre_y - group * rows_own + HALF) & (NY - 1)
    reach = jnp.where(centre_y >= 0, reach, NY)
    edges = (0, rows_own // 2, rows_own // 2 + 2 * HALF, rows_own + 2 * HALF)
    step = 256
    earlier = lax.broadcasted_iota(jnp.int32, (step, step), 0) < lax.broadcasted_iota(jnp.int32, (step, step), 1)
    tri = jnp.where(earlier, 1.0, 0.0).astype(BF16)
    marks = []
    for kind in range(3):
        inside = jnp.where((reach >= edges[kind]) & (reach < edges[kind + 1]), 1.0, 0.0)
        for part in range(total // step):
            marks.append(inside[:, part * step : (part + 1) * step])
    before = jnp.dot(jnp.concatenate(marks, axis=0).astype(BF16), tri, preferred_element_type=F32)
    rank_ref[...] = jnp.full(rank_ref.shape, -1.0, F32)
    count = jnp.zeros((groups, 1), F32)
    index = 0
    for kind in range(3):
        for part in range(total // step):
            lanes = slice(part * step, (part + 1) * step)
            found = before[index * groups : (index + 1) * groups] + count
            rank_ref[:, lanes] = jnp.where(marks[index] > 0.0, found, rank_ref[:, lanes])
            count = count + jnp.sum(marks[index], axis=1, keepdims=True)
            index += 1
        count_ref[kind] = jnp.broadcast_to(count, (groups, LANES))
    base = (round_ref[0] * SLOTS).astype(F32)
    core = place_ref[1] % 2
    high, low = split(table[...])
    both = jnp.concatenate([high, low], axis=0)
    depth = table.shape[0]
    most = jnp.max(count)
    slot = lax.broadcasted_iota(jnp.int32, (LANES, total), 0).astype(F32)
    lane = lax.broadcasted_iota(jnp.int32, (32, LANES), 1)
    rows_y = groups // 2
    for target in range(rows_y):
        own_row = pl.ds(2 * target + core, 1)
        ranks = rank_ref[own_row, :] - base
        pick = jnp.where(slot == ranks, 1.0, 0.0).astype(BF16)
        got = lax.dot_general(both, pick, NT, preferred_element_type=F32)
        got = got[0:FEAT] + got[depth : depth + FEAT]
        first = jnp.where(lane < 64, got[0:32], pltpu.roll(got[32:64], 64, 1))
        rest = [got[16 * q : 16 * q + 16] for q in range(4)]
        quarter = lane[0:16] // 32
        extra = pltpu.roll(rest[0], 64, 1)
        extra = jnp.where(quarter == 1, pltpu.roll(rest[1], 96, 1), extra)
        extra = jnp.where(quarter == 2, rest[2], extra)
        extra = jnp.where(quarter == 3, pltpu.roll(rest[3], 32, 1), extra)
        ends = [jnp.clip(count_ref[kind, own_row, :] - base, 0.0, float(SLOTS)) for kind in range(3)]
        numbers = jnp.concatenate(
            [got[TERMS : TERMS + 4], ends[2], ends[1], ends[0], jnp.full((1, LANES), most, F32)], axis=0
        )
        for copy in range(out_ref.shape[0] // (BLOCK * rows_y)):
            at = (copy * rows_y + target) * BLOCK
            out_ref[at : at + 32, :] = first
            out_ref[at + 32 : at + 48, :] = extra
            out_ref[at + 48 : at + 56, :] = numbers


def route_tiles(sources, targets, groups, place, round_index, tiles):
    return pl.pallas_call(
        functools.partial(route_kernel, sources, groups),
        in_specs=[
            pl.BlockSpec(memory_space=pltpu.SMEM),
            pl.BlockSpec(memory_space=pltpu.SMEM),
            pl.BlockSpec(memory_space=pltpu.VMEM),
        ],
        out_specs=pl.BlockSpec(memory_space=pltpu.VMEM),
        out_shape=jax.ShapeDtypeStruct((targets * BLOCK, LANES), F32),
        scratch_shapes=[
            pltpu.VMEM((sources * 16, LANES), F32),
            pltpu.VMEM((80, sources * 32), F32),
            pltpu.VMEM((groups, sources * 32), F32),
            pltpu.VMEM((3, groups, LANES), F32),
        ],
        name="route_tiles",
    )(place, round_index, tiles)


def powers_of(distance, rate):
    square = distance * distance
    envelope = jnp.where(square <= float(HALF * HALF), jnp.exp(square * rate), 0.0)
    scaled = distance * (1.0 / HALF)
    found = [envelope]
    for _ in range(NPOW - 1):
        found.append(found[-1] * scaled)
    return found


def merge_sources(sources, tiles_ref, bins, count_ref):
    lane = lax.broadcasted_iota(jnp.int32, (8, LANES), 1)
    first = LANES // 2
    counts = [tiles_ref[pl.ds(52 + k, sources, stride=BLOCK), :] for k in range(3)]
    scalars = [
        [jnp.max(count[source : source + 1, :]).astype(jnp.int32) for count in counts]
        for source in range(sources)
    ]
    for source in range(sources):
        for kind in range(3):
            count_ref[kind, source] = scalars[source][kind]
    ends = [jnp.int32(0), jnp.int32(0)]
    open_column = [[jnp.zeros((8, LANES), F32)] * (FEAT // 8) for _ in range(2)]
    for source in range(sources):
        held, upto, start = scalars[source]
        at = source * BLOCK
        pieces = [tiles_ref[at + row : at + row + 8, :] for row in range(0, 32, 8)]
        numbers = tiles_ref[at + 48 : at + 56, :]
        for half, (begin, end) in enumerate(((jnp.int32(0), upto), (start, held))):
            begin, end = jnp.minimum(begin, first), jnp.minimum(end, first)
            column = ends[half] >> 7
            offset = ends[half] & (LANES - 1)
            shift = (offset - begin) & (LANES - 1)
            after = ends[half] + (end - begin)
            kept = lane < offset
            stays = after >> 7 == column
            lower = (lane >= begin) & (lane < end)
            upper = (lane >= begin + first) & (lane < end + first)
            other = (shift + first) & (LANES - 1)
            moved = [pltpu.roll(jnp.where(lower, piece, 0.0), shift, 1) for piece in pieces]
            moved += [pltpu.roll(jnp.where(upper, piece, 0.0), other, 1) for piece in pieces]
            moved.append(pltpu.roll(jnp.where(lower, numbers, 0.0), shift, 1))
            for part, piece in enumerate(moved):
                full = jnp.where(kept, open_column[half][part], piece)
                bins[half, column, 8 * part : 8 * part + 8, :] = full
                wrapped = jnp.where(kept, piece, 0.0)
                open_column[half][part] = jnp.where(stays, full, wrapped)
            ends[half] = after
    for half in range(2):
        for part in range(FEAT // 8):
            bins[half, ends[half] >> 7, 8 * part : 8 * part + 8, :] = open_column[half][part]

    def rest(source, ends):
        at = pl.multiple_of(source * BLOCK, 8)
        held, upto, start = (count_ref[kind, source] for kind in range(3))

        def append(ends):
            numbers = tiles_ref[pl.ds(at + 48, 8), :]
            lines = [tiles_ref[pl.ds(at + 32 + row, 8), :] for row in (0, 8)]
            result = []
            for half, (begin, end) in enumerate(((jnp.int32(0), upto), (start, held))):
                begin, end = jnp.maximum(begin, first) - first, jnp.maximum(end, first) - first
                column = ends[half] >> 7
                offset = ends[half] & (LANES - 1)
                kept = lane < offset
                moved = []
                for quarter in range(4):
                    valid = (lane >= begin + 32 * quarter) & (lane < end + 32 * quarter)
                    shift = (offset - begin - 32 * quarter) & (LANES - 1)
                    moved += [pltpu.roll(jnp.where(valid, line, 0.0), shift, 1) for line in lines]
                valid = (lane >= begin + first) & (lane < end + first)
                shift = (offset - begin - first) & (LANES - 1)
                moved.append(pltpu.roll(jnp.where(valid, numbers, 0.0), shift, 1))
                for part, piece in enumerate(moved):
                    rows = slice(8 * part, 8 * part + 8)
                    bins[half, column, rows, :] = jnp.where(kept, bins[half, column, rows, :], piece)
                    bins[half, column + 1, rows, :] = jnp.where(kept, piece, 0.0)
                result.append(ends[half] + end - begin)
            return tuple(result)

        return lax.cond(held > first, append, lambda ends: ends, ends)

    return lax.fori_loop(0, sources, rest, tuple(ends))


def spectrum_kernel(
    sources, groups, kx_own, depth, later, place_ref, tiles_ref, wave, *refs
):
    if later:
        before_ref, *refs = refs
    out_ref, most_ref, bins, total, *refs = refs
    lhs_0, lhs_1, rhs_0, rhs_1, weights_0, weights_1, turn_ref, count_ref, stage, sems = refs
    rows_own = NY // groups
    rows_half = rows_own // 2
    first_kx = place_ref[0] * kx_own
    first_y = place_ref[1] * rows_own
    size = 2 * kx_own * rows_half
    scale = 1.0 / math.sqrt(NX * depth)
    kx = first_kx + lax.broadcasted_iota(jnp.int32, (kx_own, LANES), 0)
    theta = kx.astype(F32) * (2.0 * math.pi / NX)
    cosine = [None, jnp.cos(theta)]
    sine = [None, jnp.sin(theta)]
    for d in range(2, HALF + 1):
        cosine.append(cosine[-1] * cosine[1] - sine[-1] * sine[1])
        sine.append(sine[d - 1] * cosine[1] + cosine[d - 1] * sine[1])
    for d in range(1, HALF + 1):
        turn_ref[d - 1] = cosine[d]
        turn_ref[HALF + d - 1] = sine[d]
    total[1] = jnp.zeros((size, depth), F32)
    most_ref[0] = jnp.max(tiles_ref[pl.ds(55, sources, stride=BLOCK), :]).astype(jnp.int32)
    ends = merge_sources(sources, tiles_ref, bins, count_ref)
    lower = (ends[0] + LANES - 1) >> 7
    upper = jnp.maximum((ends[1] + LANES - 1) >> 7, 1)

    def build(index, lhs, rhs, weights_x):
        half = (index >= lower).astype(jnp.int32)
        block = bins.at[half, index - half * lower]
        rate = -block[TERMS : TERMS + 1, :]
        centre_x = block[TERMS + 1 : TERMS + 2, :].astype(jnp.int32)
        centre_y = block[TERMS + 2 : TERMS + 3, :].astype(jnp.int32)
        centre_z = block[TERMS + 3 : TERMS + 4, :].astype(jnp.int32)
        even_0 = jnp.full((kx_own, LANES), 0.5 * scale, F32)
        even_2 = jnp.zeros((kx_own, LANES), F32)
        odd_1 = jnp.zeros((kx_own, LANES), F32)
        odd_3 = jnp.zeros((kx_own, LANES), F32)
        for d in range(1, HALF + 1):
            scaled = d / HALF
            weight = jnp.exp(rate * float(d * d)) * scale
            even = weight * turn_ref[d - 1]
            odd = (weight * scaled) * turn_ref[HALF + d - 1]
            even_0 = even_0 + even
            even_2 = even_2 + even * (scaled * scaled)
            odd_1 = odd_1 + odd
            odd_3 = odd_3 + odd * (scaled * scaled)
        phase = ((kx * centre_x) & (NX - 1)).astype(F32) * (2.0 * math.pi / NX)
        cos_c = jnp.cos(phase) * 2.0
        sin_c = jnp.sin(phase) * 2.0
        for second in range(NPOW):
            for third in range(NPOW):
                term = second * NPOW + third
                step = NPOW * NPOW
                even = block[term : term + 1, :] * even_0
                even = even + block[2 * step + term : 2 * step + term + 1, :] * even_2
                odd = block[step + term : step + term + 1, :] * odd_1
                odd = odd + block[3 * step + term : 3 * step + term + 1, :] * odd_3
                weights_x[term, 0:kx_own, :] = cos_c * even - sin_c * odd
                weights_x[term, kx_own:, :] = -(sin_c * even + cos_c * odd)
        shift_y = centre_y - (first_y + half * rows_half + NY // 2)
        y_cells = lax.broadcasted_iota(jnp.int32, (rows_half, LANES), 0)
        off_y = ((y_cells - shift_y) & (NY - 1)).astype(F32) - float(NY // 2)
        along_y = powers_of(off_y, rate)
        for third in range(NPOW):
            for row in range(2 * kx_own):
                value = weights_x[third, row : row + 1, :] * along_y[0]
                for second in range(1, NPOW):
                    term = second * NPOW + third
                    value = value + weights_x[term, row : row + 1, :] * along_y[second]
                high, low = split(value)
                y_rows = slice(row * rows_half, (row + 1) * rows_half)
                lhs[third, y_rows, :] = high
                lhs[NPOW + third, y_rows, :] = low
        shift_z = centre_z - depth // 2
        z_cells = lax.broadcasted_iota(jnp.int32, (depth, LANES), 0)
        off_z = ((z_cells - shift_z) & (depth - 1)).astype(F32) - float(depth // 2)
        along_z = powers_of(off_z, rate)
        for third in range(NPOW):
            high, low = split(along_z[third])
            rhs[third] = high
            rhs[NPOW + third] = low

    def product(lhs, rhs):
        highs, lows = range(NPOW), range(NPOW, 2 * NPOW)
        left = jnp.concatenate([lhs[k] for k in (*highs, *lows, *highs)], axis=1)
        right = jnp.concatenate([rhs[k] for k in (*highs, *highs, *lows)], axis=1)
        return lax.dot_general(left, right, NT, preferred_element_type=F32)

    def multiply(index, lhs, rhs):
        half = (index >= lower).astype(jnp.int32)
        total[half] += product(lhs, rhs)

    def multiply_built(index, lhs, rhs):
        half = (index >= lower).astype(jnp.int32)
        total[half] = jnp.where(index >= 0, total[half] + product(lhs, rhs), 0.0)

    def two_blocks(pair, carry):
        multiply_built(2 * pair - 1, lhs_1, rhs_1)
        build(2 * pair, lhs_0, rhs_0, weights_0)
        multiply(2 * pair, lhs_0, rhs_0)
        build(2 * pair + 1, lhs_1, rhs_1, weights_1)
        return carry

    blocks = lower + upper
    lax.fori_loop(0, blocks >> 1, two_blocks, 0)

    @pl.when(blocks & 1 == 0)
    def _():
        total[1] += product(lhs_1, rhs_1)

    @pl.when(blocks & 1 == 1)
    def _():
        multiply_built(blocks - 2, lhs_1, rhs_1)
        build(blocks - 1, lhs_0, rhs_0, weights_0)
        total[1] += product(lhs_0, rhs_0)

    real_high, real_low = split(total[:, 0 : size // 2].reshape(size, depth))
    imag_high, imag_low = split(total[:, size // 2 :].reshape(size, depth))
    high = jnp.concatenate([real_high, imag_high], axis=1)
    low = jnp.concatenate([real_low, imag_low], axis=1)
    for part in range(2):
        if later:
            pltpu.sync_copy(before_ref.at[part], stage.at[part])
        columns = slice(part * depth, (part + 1) * depth)
        found = jnp.dot(high, wave[0, :, columns], preferred_element_type=F32)
        found = found + jnp.dot(low, wave[0, :, columns], preferred_element_type=F32)
        found = found + jnp.dot(high, wave[1, :, columns], preferred_element_type=F32)
        found = found.reshape(2, kx_own, rows_half, depth)
        for half in range(2):
            rows = slice(half * rows_half, (half + 1) * rows_half)
            value = found[half]
            if later:
                value = value + stage[part, :, rows, :]
            stage[part, :, rows, :] = value
        pltpu.make_async_copy(stage.at[part], out_ref.at[part], sems.at[part]).start()
    for part in range(2):
        pltpu.make_async_copy(stage.at[part], out_ref.at[part], sems.at[part]).wait()


def spectrum_of(sources, groups, kx_own, depth, place, tiles, wave, before=None):
    rows_own = NY // groups
    size = kx_own * rows_own
    columns = sources * SLOTS // LANES + 2
    vmem = pl.BlockSpec(memory_space=pltpu.VMEM)
    smem = pl.BlockSpec(memory_space=pltpu.SMEM)
    hbm = pl.BlockSpec(memory_space=pltpu.HBM)
    later = before is not None
    return pl.pallas_call(
        functools.partial(spectrum_kernel, sources, groups, kx_own, depth, later),
        in_specs=[smem, vmem, vmem] + [hbm] * later,
        out_specs=[hbm, smem],
        out_shape=[
            jax.ShapeDtypeStruct((2, kx_own, rows_own, depth), F32),
            jax.ShapeDtypeStruct((1,), jnp.int32),
        ],
        input_output_aliases={3: 0} if later else {},
        scratch_shapes=[
            pltpu.VMEM((2, columns, FEAT, LANES), F32),
            pltpu.VMEM((2, size, depth), F32),
            pltpu.VMEM((2 * NPOW, size, LANES), BF16),
            pltpu.VMEM((2 * NPOW, size, LANES), BF16),
            pltpu.VMEM((2 * NPOW, depth, LANES), BF16),
            pltpu.VMEM((2 * NPOW, depth, LANES), BF16),
            pltpu.VMEM((NPOW * NPOW, 2 * kx_own, LANES), F32),
            pltpu.VMEM((NPOW * NPOW, 2 * kx_own, LANES), F32),
            pltpu.VMEM((2 * HALF, kx_own, LANES), F32),
            pltpu.SMEM((3, sources), jnp.int32),
            pltpu.VMEM((2, kx_own, rows_own, depth), F32),
            pltpu.SemaphoreType.DMA((2,)),
        ],
        compiler_params=pltpu.CompilerParams(vmem_limit_bytes=40 * 2**20),
        name="spectrum_of_tiles",
    )(place, tiles, wave, *([before] if later else []))


def wave_table(depth):
    cells = np.arange(depth)
    angle = 2.0 * np.pi * (cells[:, None] * cells[None, :] % depth) / depth
    cosine, sine = np.cos(angle), np.sin(angle)
    table = np.block([[cosine, -sine], [sine, cosine]]).astype(np.float32)
    high = table.astype(jnp.bfloat16)
    low = (table - high.astype(np.float32)).astype(jnp.bfloat16)
    return np.stack([high, low])


def exchange(value, groups):
    return lax.all_to_all(
        value, ("slab", "grp"), split_axis=0, concat_axis=0, tiled=True, axis_index_groups=groups
    )


def local(tile_centres, tile_coeffs, tile_exponents, tile_live):
    slab_count = lax.axis_size("slab")
    grp_count = lax.axis_size("grp")
    slab, grp = lax.axis_index("slab"), lax.axis_index("grp")
    depth = CZ * slab_count
    kx_own = NX // 2 // slab_count
    count_z = slab_count // COUNT_X
    count_y = grp_count // 2

    def device(x, z, y, core):
        return (x * count_z + z) * grp_count + y * 2 + core

    xs, zs, ys, cores = range(COUNT_X), range(count_z), range(count_y), range(2)
    share = [[device(x, z, y, c) for z in zs for c in cores] for x in xs for y in ys]
    spread = [[device(x, z, y, c) for x in xs for y in ys] for z in zs for c in cores]
    sharers, chunks = len(share[0]), len(spread[0])
    place = jnp.stack([slab, grp]).astype(jnp.int32)
    wave = jnp.asarray(wave_table(depth))
    packed = pack_tiles(sharers, tile_centres, tile_coeffs, tile_exponents, tile_live)
    tiles = exchange(packed.reshape(sharers, 1, ROWS * LANES), share).reshape(sharers * ROWS, LANES)

    def one_round(index, before=None):
        routed = route_tiles(sharers, chunks, grp_count, place, index.reshape(1), tiles)
        routed = exchange(routed.reshape(chunks, BLOCK, LANES), spread).reshape(chunks * BLOCK, LANES)
        return spectrum_of(chunks, grp_count, kx_own, depth, place, routed, wave, before)

    found, most = one_round(jnp.int32(0))

    def more(state):
        return state[0] * SLOTS < state[1]

    def again(state):
        index, most, found = state
        return index + 1, most, one_round(index, found)[0]

    return lax.while_loop(more, again, (jnp.int32(1), most[0], found))[2]


def solution(mesh):
    return jax.shard_map(
        local,
        mesh=mesh,
        in_specs=(
            P(None, ("slab", "grp")),
            P(None, ("slab", "grp")),
            P(("slab", "grp")),
            P(("slab", "grp")),
        ),
        out_specs=P(None, "slab", "grp", None),
        check_vma=False,
    )
```

```python
import functools
import math

import jax
import jax.numpy as jnp
import numpy as np
from jax import lax
from jax.experimental import pallas as pl
from jax.experimental.pallas import tpu as pltpu
from jax.sharding import PartitionSpec as P

NX = 512
NY = 512
CZ = 8
HALF = 8
NPOW = 4
TERMS = NPOW * NPOW * NPOW
LANES = 128
ROWS = 17
FEAT = 72
SLOTS = 96
BLOCK = 56
COUNT_X = 4
NT = (((1,), (1,)), ((), ()))
F32 = jnp.float32
BF16 = jnp.bfloat16


def split(value):
    high = value.astype(BF16)
    return high, (value - high.astype(F32)).astype(BF16)


def pack_kernel(copies, coeffs_ref, centres_ref, exponents_ref, live_ref, out_ref, block):
    half = coeffs_ref.shape[0] // 2
    block[0:half, 0:TERMS] = coeffs_ref[0:half, :]
    block[0:half, TERMS:] = coeffs_ref[half:, :]
    centres = centres_ref[...].astype(F32)
    alive = live_ref[...] > 0
    width = 2 * half
    block[half : half + 1, 0:width] = exponents_ref[...]
    block[half : half + 1, width : 2 * width] = centres[0:1]
    block[half : half + 1, 2 * width : 3 * width] = jnp.where(alive, centres[1:2], -1.0)
    block[half : half + 1, 3 * width : 4 * width] = centres[2:3]
    value = block[...]
    for copy in range(copies):
        out_ref[copy * ROWS : (copy + 1) * ROWS, :] = value


def pack_tiles(copies, tile_centres, tile_coeffs, tile_exponents, tile_live):
    return pl.pallas_call(
        functools.partial(pack_kernel, copies),
        out_shape=jax.ShapeDtypeStruct((copies * ROWS, LANES), F32),
        scratch_shapes=[pltpu.VMEM((ROWS, LANES), F32)],
        name="pack_tiles",
    )(tile_coeffs.T, tile_centres, tile_exponents[None, :], tile_live[None, :])


def route_kernel(
    sources, groups, round_ref, tiles_ref, out_ref, rows_ref, table, rank_ref, count_ref, blocks, sem
):
    per_row = 16
    side = sources * per_row
    total = 2 * side
    for source in range(sources):
        rows_ref[source * per_row : (source + 1) * per_row, :] = tiles_ref[
            source * ROWS : source * ROWS + per_row, :
        ]
    turned = rows_ref[...].T
    table[0:TERMS, 0:side] = turned[0:TERMS]
    table[0:TERMS, side:total] = turned[TERMS:]
    misc = tiles_ref[pl.ds(per_row, sources, stride=ROWS), :]
    sublane = lax.broadcasted_iota(jnp.int32, (8, LANES), 0)
    lane = lax.broadcasted_iota(jnp.int32, (8, LANES), 1)
    own = lane // per_row == sublane
    table[TERMS:, :] = jnp.zeros((table.shape[0] - TERMS, total), F32)
    for part in range(sources // 8):
        piece = misc[part * 8 : (part + 1) * 8]
        fanned = pltpu.roll(piece, 0, 1, stride=per_row, stride_axis=0)
        for kind in range(4):
            for which in range(2):
                start = kind * 2 * per_row + which * per_row
                moved = pltpu.roll(fanned, LANES - start, 1) if start else fanned
                row = jnp.sum(jnp.where(own, moved, 0.0), axis=0, keepdims=True)
                at = which * side + part * LANES
                table[TERMS + kind : TERMS + kind + 1, at : at + LANES] = row
    centre_y = table[TERMS + 2 : TERMS + 3, :].astype(jnp.int32)
    rows_own = NY // groups
    group = lax.broadcasted_iota(jnp.int32, (groups, 1), 0)
    reach = (centre_y - group * rows_own + HALF) & (NY - 1)
    reach = jnp.where(centre_y >= 0, reach, NY)
    edges = (0, rows_own // 2, rows_own // 2 + 2 * HALF, rows_own + 2 * HALF)
    step = 256
    earlier = lax.broadcasted_iota(jnp.int32, (step, step), 0) < lax.broadcasted_iota(jnp.int32, (step, step), 1)
    tri = jnp.where(earlier, 1.0, 0.0).astype(BF16)
    marks = []
    for kind in range(3):
        inside = jnp.where((reach >= edges[kind]) & (reach < edges[kind + 1]), 1.0, 0.0)
        for part in range(total // step):
            marks.append(inside[:, part * step : (part + 1) * step])
    before = jnp.dot(jnp.concatenate(marks, axis=0).astype(BF16), tri, preferred_element_type=F32)
    rank_ref[...] = jnp.full(rank_ref.shape, -1.0, F32)
    count = jnp.zeros((groups, 1), F32)
    index = 0
    for kind in range(3):
        for part in range(total // step):
            lanes = slice(part * step, (part + 1) * step)
            found = before[index * groups : (index + 1) * groups] + count
            rank_ref[:, lanes] = jnp.where(marks[index] > 0.0, found, rank_ref[:, lanes])
            count = count + jnp.sum(marks[index], axis=1, keepdims=True)
            index += 1
        count_ref[kind] = jnp.broadcast_to(count, (groups, LANES))
    base = (round_ref[0] * SLOTS).astype(F32)
    core = lax.axis_index("grp") % 2
    high, low = split(table[...])
    both = jnp.concatenate([high, low], axis=0)
    depth = table.shape[0]
    most = jnp.max(count)
    slot = lax.broadcasted_iota(jnp.int32, (LANES, total), 0).astype(F32)
    lane = lax.broadcasted_iota(jnp.int32, (32, LANES), 1)
    rows_y = groups // 2
    copies = []
    for target in range(rows_y):
        own_row = pl.ds(2 * target + core, 1)
        ranks = rank_ref[own_row, :] - base
        pick = jnp.where(slot == ranks, 1.0, 0.0).astype(BF16)
        got = lax.dot_general(both, pick, NT, preferred_element_type=F32)
        got = got[0:FEAT] + got[depth : depth + FEAT]
        first = jnp.where(lane < 64, got[0:32], pltpu.roll(got[32:64], 64, 1))
        rest = [got[16 * q : 16 * q + 16] for q in range(4)]
        quarter = lane[0:16] // 32
        extra = pltpu.roll(rest[0], 64, 1)
        extra = jnp.where(quarter == 1, pltpu.roll(rest[1], 96, 1), extra)
        extra = jnp.where(quarter == 2, rest[2], extra)
        extra = jnp.where(quarter == 3, pltpu.roll(rest[3], 32, 1), extra)
        ends = [jnp.clip(count_ref[kind, own_row, :] - base, 0.0, float(SLOTS)) for kind in range(3)]
        numbers = jnp.concatenate(
            [got[TERMS : TERMS + 4], ends[2], ends[1], ends[0], jnp.full((1, LANES), most, F32)], axis=0
        )
        blocks[target, 0:32, :] = first
        blocks[target, 32:48, :] = extra
        blocks[target, 48:56, :] = numbers
        for copy in range(out_ref.shape[0] // rows_y):
            at = copy * rows_y + target
            copies.append(pltpu.make_async_copy(blocks.at[target], out_ref.at[at], sem.at[at]))
            copies[-1].start()
    for copy in copies:
        copy.wait()


def route_tiles(sources, targets, groups, round_index, tiles):
    return pl.pallas_call(
        functools.partial(route_kernel, sources, groups),
        in_specs=[
            pl.BlockSpec(memory_space=pltpu.SMEM),
            pl.BlockSpec(memory_space=pltpu.VMEM),
        ],
        out_specs=pl.BlockSpec(memory_space=pltpu.HBM),
        out_shape=jax.ShapeDtypeStruct((targets, BLOCK, LANES), F32),
        scratch_shapes=[
            pltpu.VMEM((sources * 16, LANES), F32),
            pltpu.VMEM((80, sources * 32), F32),
            pltpu.VMEM((groups, sources * 32), F32),
            pltpu.VMEM((3, groups, LANES), F32),
            pltpu.VMEM((groups // 2, BLOCK, LANES), F32),
            pltpu.SemaphoreType.DMA((targets,)),
        ],
        name="route_tiles",
    )(round_index, tiles)


def powers_of(distance, rate):
    square = distance * distance
    envelope = jnp.where(square <= float(HALF * HALF), jnp.exp(square * rate), 0.0)
    scaled = distance * (1.0 / HALF)
    found = [envelope]
    for _ in range(NPOW - 1):
        found.append(found[-1] * scaled)
    return found


def merge_sources(sources, tiles_ref, bins, count_ref):
    lane = lax.broadcasted_iota(jnp.int32, (8, LANES), 1)
    first = LANES // 2
    counts = [tiles_ref[pl.ds(52 + k, sources, stride=BLOCK), :] for k in range(3)]
    scalars = [
        [jnp.max(count[source : source + 1, :]).astype(jnp.int32) for count in counts]
        for source in range(sources)
    ]
    for source in range(sources):
        for kind in range(3):
            count_ref[kind, source] = scalars[source][kind]
    ends = [jnp.int32(0), jnp.int32(0)]
    open_column = [[jnp.zeros((8, LANES), F32)] * (FEAT // 8) for _ in range(2)]
    for source in range(sources):
        held, upto, start = scalars[source]
        at = source * BLOCK
        pieces = [tiles_ref[at + row : at + row + 8, :] for row in range(0, 32, 8)]
        numbers = tiles_ref[at + 48 : at + 56, :]
        for half, (begin, end) in enumerate(((jnp.int32(0), upto), (start, held))):
            begin, end = jnp.minimum(begin, first), jnp.minimum(end, first)
            column = ends[half] >> 7
            offset = ends[half] & (LANES - 1)
            shift = (offset - begin) & (LANES - 1)
            after = ends[half] + (end - begin)
            kept = lane < offset
            stays = after >> 7 == column
            lower = (lane >= begin) & (lane < end)
            upper = (lane >= begin + first) & (lane < end + first)
            other = (shift + first) & (LANES - 1)
            moved = [pltpu.roll(jnp.where(lower, piece, 0.0), shift, 1) for piece in pieces]
            moved += [pltpu.roll(jnp.where(upper, piece, 0.0), other, 1) for piece in pieces]
            moved.append(pltpu.roll(jnp.where(lower, numbers, 0.0), shift, 1))
            for part, piece in enumerate(moved):
                full = jnp.where(kept, open_column[half][part], piece)
                bins[half, column, 8 * part : 8 * part + 8, :] = full
                wrapped = jnp.where(kept, piece, 0.0)
                open_column[half][part] = jnp.where(stays, full, wrapped)
            ends[half] = after
    for half in range(2):
        for part in range(FEAT // 8):
            bins[half, ends[half] >> 7, 8 * part : 8 * part + 8, :] = open_column[half][part]

    def rest(source, ends):
        at = pl.multiple_of(source * BLOCK, 8)
        held, upto, start = (count_ref[kind, source] for kind in range(3))

        def append(ends):
            numbers = tiles_ref[pl.ds(at + 48, 8), :]
            lines = [tiles_ref[pl.ds(at + 32 + row, 8), :] for row in (0, 8)]
            result = []
            for half, (begin, end) in enumerate(((jnp.int32(0), upto), (start, held))):
                begin, end = jnp.maximum(begin, first) - first, jnp.maximum(end, first) - first
                column = ends[half] >> 7
                offset = ends[half] & (LANES - 1)
                kept = lane < offset
                moved = []
                for quarter in range(4):
                    valid = (lane >= begin + 32 * quarter) & (lane < end + 32 * quarter)
                    shift = (offset - begin - 32 * quarter) & (LANES - 1)
                    moved += [pltpu.roll(jnp.where(valid, line, 0.0), shift, 1) for line in lines]
                valid = (lane >= begin + first) & (lane < end + first)
                shift = (offset - begin - first) & (LANES - 1)
                moved.append(pltpu.roll(jnp.where(valid, numbers, 0.0), shift, 1))
                for part, piece in enumerate(moved):
                    rows = slice(8 * part, 8 * part + 8)
                    bins[half, column, rows, :] = jnp.where(kept, bins[half, column, rows, :], piece)
                    bins[half, column + 1, rows, :] = jnp.where(kept, piece, 0.0)
                result.append(ends[half] + end - begin)
            return tuple(result)

        return lax.cond(held > first, append, lambda ends: ends, ends)

    return lax.fori_loop(0, sources, rest, tuple(ends))


def spectrum_kernel(
    sources, groups, kx_own, depth, later, tiles_ref, wave, *refs
):
    if later:
        before_ref, *refs = refs
    out_ref, most_ref, bins, total, *refs = refs
    lhs, rhs, weights, turn_ref, count_ref, stage, sems = refs
    lhs, rhs, weights = ([ref.at[slot] for slot in range(4)] for ref in (lhs, rhs, weights))
    rows_own = NY // groups
    rows_half = rows_own // 2
    first_kx = lax.axis_index("slab") * kx_own
    first_y = lax.axis_index("grp") * rows_own
    size = 2 * kx_own * rows_half
    scale = 1.0 / math.sqrt(NX * depth)
    kx = first_kx + lax.broadcasted_iota(jnp.int32, (kx_own, LANES), 0)
    theta = kx.astype(F32) * (2.0 * math.pi / NX)
    cosine = [None, jnp.cos(theta)]
    sine = [None, jnp.sin(theta)]
    for d in range(2, HALF + 1):
        cosine.append(cosine[-1] * cosine[1] - sine[-1] * sine[1])
        sine.append(sine[d - 1] * cosine[1] + cosine[d - 1] * sine[1])
    for d in range(1, HALF + 1):
        turn_ref[d - 1] = cosine[d]
        turn_ref[HALF + d - 1] = sine[d]
    total[...] = jnp.zeros_like(total)
    most_ref[0] = jnp.max(tiles_ref[pl.ds(55, sources, stride=BLOCK), :]).astype(jnp.int32)
    ends = merge_sources(sources, tiles_ref, bins, count_ref)
    lower = (ends[0] + LANES - 1) >> 7
    upper = (ends[1] + LANES - 1) >> 7

    def build(index, lhs, rhs, weights_x):
        half = (index >= lower).astype(jnp.int32)
        block = bins.at[half, index - half * lower]
        rate = -block[TERMS : TERMS + 1, :]
        centre_x = block[TERMS + 1 : TERMS + 2, :].astype(jnp.int32)
        centre_y = block[TERMS + 2 : TERMS + 3, :].astype(jnp.int32)
        centre_z = block[TERMS + 3 : TERMS + 4, :].astype(jnp.int32)
        even_0 = jnp.full((kx_own, LANES), 0.5 * scale, F32)
        even_2 = jnp.zeros((kx_own, LANES), F32)
        odd_1 = jnp.zeros((kx_own, LANES), F32)
        odd_3 = jnp.zeros((kx_own, LANES), F32)
        for d in range(1, HALF + 1):
            scaled = d / HALF
            weight = jnp.exp(rate * float(d * d)) * scale
            even = weight * turn_ref[d - 1]
            odd = (weight * scaled) * turn_ref[HALF + d - 1]
            even_0 = even_0 + even
            even_2 = even_2 + even * (scaled * scaled)
            odd_1 = odd_1 + odd
            odd_3 = odd_3 + odd * (scaled * scaled)
        phase = ((kx * centre_x) & (NX - 1)).astype(F32) * (2.0 * math.pi / NX)
        cos_c = jnp.cos(phase) * 2.0
        sin_c = jnp.sin(phase) * 2.0
        for second in range(NPOW):
            for third in range(NPOW):
                term = second * NPOW + third
                step = NPOW * NPOW
                even = block[term : term + 1, :] * even_0
                even = even + block[2 * step + term : 2 * step + term + 1, :] * even_2
                odd = block[step + term : step + term + 1, :] * odd_1
                odd = odd + block[3 * step + term : 3 * step + term + 1, :] * odd_3
                weights_x[term, 0:kx_own, :] = cos_c * even - sin_c * odd
                weights_x[term, kx_own:, :] = -(sin_c * even + cos_c * odd)
        shift_y = centre_y - (first_y + half * rows_half + NY // 2)
        y_cells = lax.broadcasted_iota(jnp.int32, (rows_half, LANES), 0)
        off_y = ((y_cells - shift_y) & (NY - 1)).astype(F32) - float(NY // 2)
        along_y = powers_of(off_y, rate)
        for third in range(NPOW):
            for row in range(2 * kx_own):
                value = weights_x[third, row : row + 1, :] * along_y[0]
                for second in range(1, NPOW):
                    term = second * NPOW + third
                    value = value + weights_x[term, row : row + 1, :] * along_y[second]
                high, low = split(value)
                y_rows = slice(row * rows_half, (row + 1) * rows_half)
                lhs[third, y_rows, :] = high
                lhs[NPOW + third, y_rows, :] = low
        shift_z = centre_z - depth // 2
        z_cells = lax.broadcasted_iota(jnp.int32, (depth, LANES), 0)
        off_z = ((z_cells - shift_z) & (depth - 1)).astype(F32) - float(depth // 2)
        along_z = powers_of(off_z, rate)
        for third in range(NPOW):
            high, low = split(along_z[third])
            rhs[third] = high
            rhs[NPOW + third] = low

    def product(lhs, rhs):
        highs, lows = range(NPOW), range(NPOW, 2 * NPOW)
        left = jnp.concatenate([lhs[k] for k in (*highs, *lows, *highs)], axis=1)
        right = jnp.concatenate([rhs[k] for k in (*highs, *highs, *lows)], axis=1)
        return lax.dot_general(left, right, NT, preferred_element_type=F32)

    def multiply(index, slot):
        half = (index >= lower).astype(jnp.int32)
        total[half] += product(lhs[slot], rhs[slot])

    def four_blocks(four, carry):
        half = (4 * four - 1 >= lower).astype(jnp.int32)
        total[half] += jnp.where(four > 0, product(lhs[3], rhs[3]), 0.0)
        for slot in range(4):
            build(4 * four + slot, lhs[slot], rhs[slot], weights[slot])
            if slot < 3:
                multiply(4 * four + slot, slot)
        return carry

    def one_block(index, carry):
        build(index, lhs[0], rhs[0], weights[0])
        multiply(index, 0)
        return carry

    blocks = lower + upper
    built = jnp.int32(0)
    if not later:
        built = (blocks >> 2) * 4
        lax.fori_loop(0, blocks >> 2, four_blocks, 0)

        @pl.when(built > 0)
        def _():
            multiply(built - 1, 3)

    lax.fori_loop(built, blocks, one_block, 0)
    real_high, real_low = split(total[:, 0 : size // 2].reshape(size, depth))
    imag_high, imag_low = split(total[:, size // 2 :].reshape(size, depth))
    spectra = jnp.concatenate(
        [real_high, imag_high, real_low, imag_low, real_high, imag_high], axis=1
    )
    waves = jnp.concatenate([wave[0], wave[0], wave[1]], axis=0)
    found = jnp.dot(spectra, waves, preferred_element_type=F32)
    found = found.reshape(2, kx_own, rows_half, 2 * depth)
    if later:
        pltpu.sync_copy(before_ref, stage)
    for part in range(2):
        for half in range(2):
            rows = slice(half * rows_half, (half + 1) * rows_half)
            value = found[half, :, :, part * depth : (part + 1) * depth]
            if later:
                value = value + stage[part, :, rows, :]
            stage[part, :, rows, :] = value
        pltpu.make_async_copy(stage.at[part], out_ref.at[part], sems.at[part]).start()
    for part in range(2):
        pltpu.make_async_copy(stage.at[part], out_ref.at[part], sems.at[part]).wait()


def spectrum_of(sources, groups, kx_own, depth, tiles, wave, before=None):
    rows_own = NY // groups
    size = kx_own * rows_own
    columns = sources * SLOTS // LANES + 2
    vmem = pl.BlockSpec(memory_space=pltpu.VMEM)
    smem = pl.BlockSpec(memory_space=pltpu.SMEM)
    hbm = pl.BlockSpec(memory_space=pltpu.HBM)
    later = before is not None
    return pl.pallas_call(
        functools.partial(spectrum_kernel, sources, groups, kx_own, depth, later),
        in_specs=[vmem, vmem] + [hbm] * later,
        out_specs=[hbm, smem],
        out_shape=[
            jax.ShapeDtypeStruct((2, kx_own, rows_own, depth), F32),
            jax.ShapeDtypeStruct((1,), jnp.int32),
        ],
        input_output_aliases={2: 0} if later else {},
        scratch_shapes=[
            pltpu.VMEM((2, columns, FEAT, LANES), F32),
            pltpu.VMEM((2, size, depth), F32),
            pltpu.VMEM((4, 2 * NPOW, size, LANES), BF16),
            pltpu.VMEM((4, 2 * NPOW, depth, LANES), BF16),
            pltpu.VMEM((4, NPOW * NPOW, 2 * kx_own, LANES), F32),
            pltpu.VMEM((2 * HALF, kx_own, LANES), F32),
            pltpu.SMEM((3, sources), jnp.int32),
            pltpu.VMEM((2, kx_own, rows_own, depth), F32),
            pltpu.SemaphoreType.DMA((2,)),
        ],
        compiler_params=pltpu.CompilerParams(vmem_limit_bytes=40 * 2**20),
        name="spectrum_of_tiles",
    )(tiles, wave, *([before] if later else []))


def wave_table(depth):
    cells = np.arange(depth)
    angle = 2.0 * np.pi * (cells[:, None] * cells[None, :] % depth) / depth
    cosine, sine = np.cos(angle), np.sin(angle)
    table = np.block([[cosine, -sine], [sine, cosine]]).astype(np.float32)
    high = table.astype(jnp.bfloat16)
    low = (table - high.astype(np.float32)).astype(jnp.bfloat16)
    return np.stack([high, low])


def exchange(value, groups):
    return lax.all_to_all(
        value, ("slab", "grp"), split_axis=0, concat_axis=0, tiled=True, axis_index_groups=groups
    )


def local(tile_centres, tile_coeffs, tile_exponents, tile_live):
    slab_count = lax.axis_size("slab")
    grp_count = lax.axis_size("grp")
    depth = CZ * slab_count
    kx_own = NX // 2 // slab_count
    count_z = slab_count // COUNT_X
    count_y = grp_count // 2

    def device(x, z, y, core):
        return (x * count_z + z) * grp_count + y * 2 + core

    xs, zs, ys, cores = range(COUNT_X), range(count_z), range(count_y), range(2)
    share = [[device(x, z, y, c) for z in zs for c in cores] for x in xs for y in ys]
    spread = [[device(x, z, y, c) for x in xs for y in ys] for z in zs for c in cores]
    sharers, chunks = len(share[0]), len(spread[0])
    wave = jnp.asarray(wave_table(depth))
    packed = pack_tiles(sharers, tile_centres, tile_coeffs, tile_exponents, tile_live)
    tiles = exchange(packed.reshape(sharers, 1, ROWS * LANES), share).reshape(sharers * ROWS, LANES)

    def one_round(index, before=None):
        routed = route_tiles(sharers, chunks, grp_count, index.reshape(1), tiles)
        routed = exchange(routed, spread).reshape(chunks * BLOCK, LANES)
        return spectrum_of(chunks, grp_count, kx_own, depth, routed, wave, before)

    found, most = one_round(jnp.int32(0))

    def more(state):
        return state[0] * SLOTS < state[1]

    def again(state):
        index, most, found = state
        return index + 1, most, one_round(index, found)[0]

    return lax.while_loop(more, again, (jnp.int32(1), most[0], found))[2]


def solution(mesh):
    return jax.shard_map(
        local,
        mesh=mesh,
        in_specs=(
            P(None, ("slab", "grp")),
            P(None, ("slab", "grp")),
            P(("slab", "grp")),
            P(("slab", "grp")),
        ),
        out_specs=P(None, "slab", "grp", None),
        check_vma=False,
    )
```

```python
import functools
import math

import jax
import jax.numpy as jnp
import numpy as np
from jax import lax
from jax.experimental import pallas as pl
from jax.experimental.pallas import tpu as pltpu
from jax.sharding import PartitionSpec as P

NX = 512
NY = 512
CZ = 8
HALF = 8
NPOW = 4
TERMS = NPOW * NPOW * NPOW
LANES = 128
ROWS = 17
FEAT = 72
SLOTS = 96
BLOCK = 56
COUNT_X = 4
NT = (((1,), (1,)), ((), ()))
F32 = jnp.float32
BF16 = jnp.bfloat16


def split(value):
    high = value.astype(BF16)
    return high, (value - high.astype(F32)).astype(BF16)


def pack_kernel(copies, coeffs_ref, centres_ref, exponents_ref, live_ref, out_ref, block):
    half = coeffs_ref.shape[0] // 2
    block[0:half, 0:TERMS] = coeffs_ref[0:half, :]
    block[0:half, TERMS:] = coeffs_ref[half:, :]
    centres = centres_ref[...].astype(F32)
    alive = live_ref[...] > 0
    width = 2 * half
    block[half : half + 1, 0:width] = exponents_ref[...]
    block[half : half + 1, width : 2 * width] = centres[0:1]
    block[half : half + 1, 2 * width : 3 * width] = jnp.where(alive, centres[1:2], -1.0)
    block[half : half + 1, 3 * width : 4 * width] = centres[2:3]
    value = block[...]
    for copy in range(copies):
        out_ref[copy * ROWS : (copy + 1) * ROWS, :] = value


def pack_tiles(copies, tile_centres, tile_coeffs, tile_exponents, tile_live):
    return pl.pallas_call(
        functools.partial(pack_kernel, copies),
        out_shape=jax.ShapeDtypeStruct((copies * ROWS, LANES), F32),
        scratch_shapes=[pltpu.VMEM((ROWS, LANES), F32)],
        name="pack_tiles",
    )(tile_coeffs.T, tile_centres, tile_exponents[None, :], tile_live[None, :])


def route_kernel(
    sources, groups, round_ref, tiles_ref, out_ref, rows_ref, table, rank_ref, count_ref, blocks, sem
):
    per_row = 16
    side = sources * per_row
    total = 2 * side
    for source in range(sources):
        rows_ref[source * per_row : (source + 1) * per_row, :] = tiles_ref[
            source * ROWS : source * ROWS + per_row, :
        ]
    turned = rows_ref[...].T
    table[0:TERMS, 0:side] = turned[0:TERMS]
    table[0:TERMS, side:total] = turned[TERMS:]
    misc = tiles_ref[pl.ds(per_row, sources, stride=ROWS), :]
    sublane = lax.broadcasted_iota(jnp.int32, (8, LANES), 0)
    lane = lax.broadcasted_iota(jnp.int32, (8, LANES), 1)
    own = lane // per_row == sublane
    table[TERMS:, :] = jnp.zeros((table.shape[0] - TERMS, total), F32)
    for part in range(sources // 8):
        piece = misc[part * 8 : (part + 1) * 8]
        fanned = pltpu.roll(piece, 0, 1, stride=per_row, stride_axis=0)
        for kind in range(4):
            for which in range(2):
                start = kind * 2 * per_row + which * per_row
                moved = pltpu.roll(fanned, LANES - start, 1) if start else fanned
                row = jnp.sum(jnp.where(own, moved, 0.0), axis=0, keepdims=True)
                at = which * side + part * LANES
                table[TERMS + kind : TERMS + kind + 1, at : at + LANES] = row
    centre_y = table[TERMS + 2 : TERMS + 3, :].astype(jnp.int32)
    rows_own = NY // groups
    group = lax.broadcasted_iota(jnp.int32, (groups, 1), 0)
    reach = (centre_y - group * rows_own + HALF) & (NY - 1)
    reach = jnp.where(centre_y >= 0, reach, NY)
    edges = (0, rows_own // 2, rows_own // 2 + 2 * HALF, rows_own + 2 * HALF)
    step = 256
    earlier = lax.broadcasted_iota(jnp.int32, (step, step), 0) < lax.broadcasted_iota(jnp.int32, (step, step), 1)
    tri = jnp.where(earlier, 1.0, 0.0).astype(BF16)
    marks = []
    for kind in range(3):
        inside = jnp.where((reach >= edges[kind]) & (reach < edges[kind + 1]), 1.0, 0.0)
        for part in range(total // step):
            marks.append(inside[:, part * step : (part + 1) * step])
    before = jnp.dot(jnp.concatenate(marks, axis=0).astype(BF16), tri, preferred_element_type=F32)
    rank_ref[...] = jnp.full(rank_ref.shape, -1.0, F32)
    count = jnp.zeros((groups, 1), F32)
    index = 0
    for kind in range(3):
        for part in range(total // step):
            lanes = slice(part * step, (part + 1) * step)
            found = before[index * groups : (index + 1) * groups] + count
            rank_ref[:, lanes] = jnp.where(marks[index] > 0.0, found, rank_ref[:, lanes])
            count = count + jnp.sum(marks[index], axis=1, keepdims=True)
            index += 1
        count_ref[kind] = jnp.broadcast_to(count, (groups, LANES))
    base = (round_ref[0] * SLOTS).astype(F32)
    core = lax.axis_index("grp") % 2
    high, low = split(table[...])
    both = jnp.concatenate([high, low], axis=0)
    depth = table.shape[0]
    most = jnp.max(count)
    slot = lax.broadcasted_iota(jnp.int32, (LANES, total), 0).astype(F32)
    lane = lax.broadcasted_iota(jnp.int32, (32, LANES), 1)
    rows_y = groups // 2
    copies = []
    for target in range(rows_y):
        own_row = pl.ds(2 * target + core, 1)
        ranks = rank_ref[own_row, :] - base
        pick = jnp.where(slot == ranks, 1.0, 0.0).astype(BF16)
        got = lax.dot_general(both, pick, NT, preferred_element_type=F32)
        got = got[0:FEAT] + got[depth : depth + FEAT]
        first = jnp.where(lane < 64, got[0:32], pltpu.roll(got[32:64], 64, 1))
        rest = [got[16 * q : 16 * q + 16] for q in range(4)]
        quarter = lane[0:16] // 32
        extra = pltpu.roll(rest[0], 64, 1)
        extra = jnp.where(quarter == 1, pltpu.roll(rest[1], 96, 1), extra)
        extra = jnp.where(quarter == 2, rest[2], extra)
        extra = jnp.where(quarter == 3, pltpu.roll(rest[3], 32, 1), extra)
        ends = [jnp.clip(count_ref[kind, own_row, :] - base, 0.0, float(SLOTS)) for kind in range(3)]
        numbers = jnp.concatenate(
            [got[TERMS : TERMS + 4], ends[2], ends[1], ends[0], jnp.full((1, LANES), most, F32)], axis=0
        )
        blocks[target, 0:32, :] = first
        blocks[target, 32:48, :] = extra
        blocks[target, 48:56, :] = numbers
        for copy in range(out_ref.shape[0] // rows_y):
            at = copy * rows_y + target
            copies.append(pltpu.make_async_copy(blocks.at[target], out_ref.at[at], sem.at[at]))
            copies[-1].start()
    for copy in copies:
        copy.wait()


def route_tiles(sources, targets, groups, round_index, tiles):
    return pl.pallas_call(
        functools.partial(route_kernel, sources, groups),
        in_specs=[
            pl.BlockSpec(memory_space=pltpu.SMEM),
            pl.BlockSpec(memory_space=pltpu.VMEM),
        ],
        out_specs=pl.BlockSpec(memory_space=pltpu.HBM),
        out_shape=jax.ShapeDtypeStruct((targets, BLOCK, LANES), F32),
        scratch_shapes=[
            pltpu.VMEM((sources * 16, LANES), F32),
            pltpu.VMEM((80, sources * 32), F32),
            pltpu.VMEM((groups, sources * 32), F32),
            pltpu.VMEM((3, groups, LANES), F32),
            pltpu.VMEM((groups // 2, BLOCK, LANES), F32),
            pltpu.SemaphoreType.DMA((targets,)),
        ],
        name="route_tiles",
    )(round_index, tiles)


def powers_of(distance, rate):
    square = distance * distance
    envelope = jnp.where(square <= float(HALF * HALF), jnp.exp(square * rate), 0.0)
    scaled = distance * (1.0 / HALF)
    found = [envelope]
    for _ in range(NPOW - 1):
        found.append(found[-1] * scaled)
    return found


def merge_sources(sources, tiles_ref, bins, count_ref):
    lane = lax.broadcasted_iota(jnp.int32, (8, LANES), 1)
    first = LANES // 2
    counts = [tiles_ref[pl.ds(52 + k, sources, stride=BLOCK), :] for k in range(3)]
    scalars = [
        [jnp.max(count[source : source + 1, :]).astype(jnp.int32) for count in counts]
        for source in range(sources)
    ]
    for source in range(sources):
        for kind in range(3):
            count_ref[kind, source] = scalars[source][kind]
    ends = [jnp.int32(0), jnp.int32(0)]
    open_column = [[jnp.zeros((8, LANES), F32)] * (FEAT // 8) for _ in range(2)]
    for source in range(sources):
        held, upto, start = scalars[source]
        at = source * BLOCK
        pieces = [tiles_ref[at + row : at + row + 8, :] for row in range(0, 32, 8)]
        numbers = tiles_ref[at + 48 : at + 56, :]
        for half, (begin, end) in enumerate(((jnp.int32(0), upto), (start, held))):
            begin, end = jnp.minimum(begin, first), jnp.minimum(end, first)
            column = ends[half] >> 7
            offset = ends[half] & (LANES - 1)
            shift = (offset - begin) & (LANES - 1)
            after = ends[half] + (end - begin)
            kept = lane < offset
            stays = after >> 7 == column
            lower = (lane >= begin) & (lane < end)
            upper = (lane >= begin + first) & (lane < end + first)
            other = (shift + first) & (LANES - 1)
            moved = [pltpu.roll(jnp.where(lower, piece, 0.0), shift, 1) for piece in pieces]
            moved += [pltpu.roll(jnp.where(upper, piece, 0.0), other, 1) for piece in pieces]
            moved.append(pltpu.roll(jnp.where(lower, numbers, 0.0), shift, 1))
            for part, piece in enumerate(moved):
                full = jnp.where(kept, open_column[half][part], piece)
                bins[half, column, 8 * part : 8 * part + 8, :] = full
                wrapped = jnp.where(kept, piece, 0.0)
                open_column[half][part] = jnp.where(stays, full, wrapped)
            ends[half] = after
    for half in range(2):
        for part in range(FEAT // 8):
            bins[half, ends[half] >> 7, 8 * part : 8 * part + 8, :] = open_column[half][part]

    def rest(source, ends):
        at = pl.multiple_of(source * BLOCK, 8)
        held, upto, start = (count_ref[kind, source] for kind in range(3))

        def append(ends):
            numbers = tiles_ref[pl.ds(at + 48, 8), :]
            lines = [tiles_ref[pl.ds(at + 32 + row, 8), :] for row in (0, 8)]
            result = []
            for half, (begin, end) in enumerate(((jnp.int32(0), upto), (start, held))):
                begin, end = jnp.maximum(begin, first) - first, jnp.maximum(end, first) - first
                column = ends[half] >> 7
                offset = ends[half] & (LANES - 1)
                kept = lane < offset
                moved = []
                for quarter in range(4):
                    valid = (lane >= begin + 32 * quarter) & (lane < end + 32 * quarter)
                    shift = (offset - begin - 32 * quarter) & (LANES - 1)
                    moved += [pltpu.roll(jnp.where(valid, line, 0.0), shift, 1) for line in lines]
                valid = (lane >= begin + first) & (lane < end + first)
                shift = (offset - begin - first) & (LANES - 1)
                moved.append(pltpu.roll(jnp.where(valid, numbers, 0.0), shift, 1))
                for part, piece in enumerate(moved):
                    rows = slice(8 * part, 8 * part + 8)
                    bins[half, column, rows, :] = jnp.where(kept, bins[half, column, rows, :], piece)
                    bins[half, column + 1, rows, :] = jnp.where(kept, piece, 0.0)
                result.append(ends[half] + end - begin)
            return tuple(result)

        return lax.cond(held > first, append, lambda ends: ends, ends)

    return lax.fori_loop(0, sources, rest, tuple(ends))


def spectrum_kernel(
    sources, groups, kx_own, depth, later, tiles_ref, wave, *refs
):
    if later:
        before_ref, *refs = refs
    out_ref, most_ref, bins, total, *refs = refs
    lhs, rhs, weights, turn_ref, count_ref, planes_ref, stage, sems = refs
    lhs, rhs, weights = ([ref.at[slot] for slot in range(4)] for ref in (lhs, rhs, weights))
    rows_own = NY // groups
    rows_half = rows_own // 2
    first_kx = lax.axis_index("slab") * kx_own
    first_y = lax.axis_index("grp") * rows_own
    size = 2 * kx_own * rows_half
    scale = 1.0 / math.sqrt(NX * depth)
    kx = first_kx + lax.broadcasted_iota(jnp.int32, (kx_own, LANES), 0)
    theta = kx.astype(F32) * (2.0 * math.pi / NX)
    cosine = [None, jnp.cos(theta)]
    sine = [None, jnp.sin(theta)]
    for d in range(2, HALF + 1):
        cosine.append(cosine[-1] * cosine[1] - sine[-1] * sine[1])
        sine.append(sine[d - 1] * cosine[1] + cosine[d - 1] * sine[1])
    for d in range(1, HALF + 1):
        turn_ref[d - 1] = cosine[d]
        turn_ref[HALF + d - 1] = sine[d]
    total[...] = jnp.zeros_like(total)
    place = lax.broadcasted_iota(jnp.int32, (depth, LANES), 0)
    planes_ref[...] = jnp.where(place < depth // 2, 2 * place, 2 * place + 1 - depth)
    most_ref[0] = jnp.max(tiles_ref[pl.ds(55, sources, stride=BLOCK), :]).astype(jnp.int32)
    ends = merge_sources(sources, tiles_ref, bins, count_ref)
    lower = (ends[0] + LANES - 1) >> 7
    upper = (ends[1] + LANES - 1) >> 7

    def build(index, lhs, rhs, weights_x):
        half = (index >= lower).astype(jnp.int32)
        block = bins.at[half, index - half * lower]
        rate = -block[TERMS : TERMS + 1, :]
        centre_x = block[TERMS + 1 : TERMS + 2, :].astype(jnp.int32)
        centre_y = block[TERMS + 2 : TERMS + 3, :].astype(jnp.int32)
        centre_z = block[TERMS + 3 : TERMS + 4, :].astype(jnp.int32)
        even_0 = jnp.full((kx_own, LANES), 0.5 * scale, F32)
        even_2 = jnp.zeros((kx_own, LANES), F32)
        odd_1 = jnp.zeros((kx_own, LANES), F32)
        odd_3 = jnp.zeros((kx_own, LANES), F32)
        for d in range(1, HALF + 1):
            scaled = d / HALF
            weight = jnp.exp(rate * float(d * d)) * scale
            even = weight * turn_ref[d - 1]
            odd = (weight * scaled) * turn_ref[HALF + d - 1]
            even_0 = even_0 + even
            even_2 = even_2 + even * (scaled * scaled)
            odd_1 = odd_1 + odd
            odd_3 = odd_3 + odd * (scaled * scaled)
        phase = ((kx * centre_x) & (NX - 1)).astype(F32) * (2.0 * math.pi / NX)
        cos_c = jnp.cos(phase) * 2.0
        sin_c = jnp.sin(phase) * 2.0
        for second in range(NPOW):
            for third in range(NPOW):
                term = second * NPOW + third
                step = NPOW * NPOW
                even = block[term : term + 1, :] * even_0
                even = even + block[2 * step + term : 2 * step + term + 1, :] * even_2
                odd = block[step + term : step + term + 1, :] * odd_1
                odd = odd + block[3 * step + term : 3 * step + term + 1, :] * odd_3
                weights_x[term, 0:kx_own, :] = cos_c * even - sin_c * odd
                weights_x[term, kx_own:, :] = -(sin_c * even + cos_c * odd)
        shift_y = centre_y - (first_y + half * rows_half + NY // 2)
        y_cells = lax.broadcasted_iota(jnp.int32, (rows_half, LANES), 0)
        off_y = ((y_cells - shift_y) & (NY - 1)).astype(F32) - float(NY // 2)
        along_y = powers_of(off_y, rate)
        for third in range(NPOW):
            for row in range(2 * kx_own):
                value = weights_x[third, row : row + 1, :] * along_y[0]
                for second in range(1, NPOW):
                    term = second * NPOW + third
                    value = value + weights_x[term, row : row + 1, :] * along_y[second]
                high, low = split(value)
                y_rows = slice(row * rows_half, (row + 1) * rows_half)
                lhs[third, y_rows, :] = high
                lhs[NPOW + third, y_rows, :] = low
        shift_z = centre_z - depth // 2
        off_z = ((planes_ref[...] - shift_z) & (depth - 1)).astype(F32) - float(depth // 2)
        along_z = powers_of(off_z, rate)
        for third in range(NPOW):
            high, low = split(along_z[third])
            rhs[third] = high
            rhs[NPOW + third] = low

    def product(lhs, rhs):
        highs, lows = range(NPOW), range(NPOW, 2 * NPOW)
        left = jnp.concatenate([lhs[k] for k in (*highs, *lows, *highs)], axis=1)
        right = jnp.concatenate([rhs[k] for k in (*highs, *highs, *lows)], axis=1)
        return lax.dot_general(left, right, NT, preferred_element_type=F32)

    def multiply(index, slot):
        half = (index >= lower).astype(jnp.int32)
        total[half] += product(lhs[slot], rhs[slot])

    def four_blocks(four, carry):
        half = (4 * four - 1 >= lower).astype(jnp.int32)
        total[half] += jnp.where(four > 0, product(lhs[3], rhs[3]), 0.0)
        for slot in range(4):
            build(4 * four + slot, lhs[slot], rhs[slot], weights[slot])
            if slot < 3:
                multiply(4 * four + slot, slot)
        return carry

    def one_block(index, carry):
        build(index, lhs[0], rhs[0], weights[0])
        multiply(index, 0)
        return carry

    blocks = lower + upper
    built = jnp.int32(0)
    if not later:
        built = (blocks >> 2) * 4
        lax.fori_loop(0, blocks >> 2, four_blocks, 0)

        @pl.when(built > 0)
        def _():
            multiply(built - 1, 3)

    lax.fori_loop(built, blocks, one_block, 0)
    real_high, real_low = split(total[:, 0 : size // 2].reshape(size, depth))
    imag_high, imag_low = split(total[:, size // 2 :].reshape(size, depth))
    sums = []
    for parity in range(2):
        planes = slice(parity * (depth // 2), (parity + 1) * (depth // 2))
        high = [real_high[:, planes], imag_high[:, planes]]
        low = [real_low[:, planes], imag_low[:, planes]]
        spectra = jnp.concatenate([*high, *low, *high], axis=1)
        waves = jnp.concatenate([wave[0, parity], wave[0, parity], wave[1, parity]], axis=0)
        sums.append(jnp.dot(spectra, waves, preferred_element_type=F32))
    found = [sums[0] + sums[1], sums[0] - sums[1]]
    if later:
        pltpu.sync_copy(before_ref, stage)
    for part in range(2):
        for half in range(2):
            rows = slice(half * rows_half, (half + 1) * rows_half)
            for upper_half in range(2):
                columns = slice(upper_half * (depth // 2), (upper_half + 1) * (depth // 2))
                value = found[upper_half][
                    half * (size // 2) : (half + 1) * (size // 2),
                    part * (depth // 2) : (part + 1) * (depth // 2),
                ].reshape(kx_own, rows_half, depth // 2)
                if later:
                    value = value + stage[part, :, rows, columns]
                stage[part, :, rows, columns] = value
        pltpu.make_async_copy(stage.at[part], out_ref.at[part], sems.at[part]).start()
    for part in range(2):
        pltpu.make_async_copy(stage.at[part], out_ref.at[part], sems.at[part]).wait()


def spectrum_of(sources, groups, kx_own, depth, tiles, wave, before=None):
    rows_own = NY // groups
    size = kx_own * rows_own
    columns = sources * SLOTS // LANES + 2
    vmem = pl.BlockSpec(memory_space=pltpu.VMEM)
    smem = pl.BlockSpec(memory_space=pltpu.SMEM)
    hbm = pl.BlockSpec(memory_space=pltpu.HBM)
    later = before is not None
    return pl.pallas_call(
        functools.partial(spectrum_kernel, sources, groups, kx_own, depth, later),
        in_specs=[vmem, vmem] + [hbm] * later,
        out_specs=[hbm, smem],
        out_shape=[
            jax.ShapeDtypeStruct((2, kx_own, rows_own, depth), F32),
            jax.ShapeDtypeStruct((1,), jnp.int32),
        ],
        input_output_aliases={2: 0} if later else {},
        scratch_shapes=[
            pltpu.VMEM((2, columns, FEAT, LANES), F32),
            pltpu.VMEM((2, size, depth), F32),
            pltpu.VMEM((4, 2 * NPOW, size, LANES), BF16),
            pltpu.VMEM((4, 2 * NPOW, depth, LANES), BF16),
            pltpu.VMEM((4, NPOW * NPOW, 2 * kx_own, LANES), F32),
            pltpu.VMEM((2 * HALF, kx_own, LANES), F32),
            pltpu.SMEM((3, sources), jnp.int32),
            pltpu.VMEM((depth, LANES), jnp.int32),
            pltpu.VMEM((2, kx_own, rows_own, depth), F32),
            pltpu.SemaphoreType.DMA((2,)),
        ],
        compiler_params=pltpu.CompilerParams(vmem_limit_bytes=40 * 2**20),
        name="spectrum_of_tiles",
    )(tiles, wave, *([before] if later else []))


def wave_table(depth):
    cells = np.arange(depth)
    angle = 2.0 * np.pi * (cells[:, None] * cells[None, : depth // 2] % depth) / depth
    cosine, sine = np.cos(angle), np.sin(angle)
    tables = []
    for parity in range(2):
        c, s = cosine[parity::2], sine[parity::2]
        tables.append(np.block([[c, -s], [s, c]]))
    table = np.stack(tables).astype(np.float32)
    high = table.astype(jnp.bfloat16)
    low = (table - high.astype(np.float32)).astype(jnp.bfloat16)
    return np.stack([high, low])


def exchange(value, groups):
    return lax.all_to_all(
        value, ("slab", "grp"), split_axis=0, concat_axis=0, tiled=True, axis_index_groups=groups
    )


def local(tile_centres, tile_coeffs, tile_exponents, tile_live):
    slab_count = lax.axis_size("slab")
    grp_count = lax.axis_size("grp")
    depth = CZ * slab_count
    kx_own = NX // 2 // slab_count
    count_z = slab_count // COUNT_X
    count_y = grp_count // 2

    def device(x, z, y, core):
        return (x * count_z + z) * grp_count + y * 2 + core

    xs, zs, ys, cores = range(COUNT_X), range(count_z), range(count_y), range(2)
    share = [[device(x, z, y, c) for z in zs for c in cores] for x in xs for y in ys]
    spread = [[device(x, z, y, c) for x in xs for y in ys] for z in zs for c in cores]
    sharers, chunks = len(share[0]), len(spread[0])
    wave = jnp.asarray(wave_table(depth))
    packed = pack_tiles(sharers, tile_centres, tile_coeffs, tile_exponents, tile_live)
    tiles = exchange(packed.reshape(sharers, 1, ROWS * LANES), share).reshape(sharers * ROWS, LANES)

    def one_round(index, before=None):
        routed = route_tiles(sharers, chunks, grp_count, index.reshape(1), tiles)
        routed = exchange(routed, spread).reshape(chunks * BLOCK, LANES)
        return spectrum_of(chunks, grp_count, kx_own, depth, routed, wave, before)

    found, most = one_round(jnp.int32(0))

    def more(state):
        return state[0] * SLOTS < state[1]

    def again(state):
        index, most, found = state
        return index + 1, most, one_round(index, found)[0]

    return lax.while_loop(more, again, (jnp.int32(1), most[0], found))[2]


def solution(mesh):
    return jax.shard_map(
        local,
        mesh=mesh,
        in_specs=(
            P(None, ("slab", "grp")),
            P(None, ("slab", "grp")),
            P(("slab", "grp")),
            P(("slab", "grp")),
        ),
        out_specs=P(None, "slab", "grp", None),
        check_vma=False,
    )
```
